32 devices in a mesh: groups: 2 (over y), seq: 16 (over z, x, core).
Axes of the slice: x: 2, y: 2, z: 4, core: 2. Of those that a mesh axis runs over, the one named last changes fastest.
Arguments:
- inputs: bfloat16 [16384, 768], P(('groups', 'seq')), parts along dimension 0, may hold values from -400 to 400
- projection: bfloat16 [768, 2304], P('seq'), may hold values from -2 to 2
- positions: int32 [16384], P(('groups', 'seq')), parts along dimension 0, may hold values from 0 to 1024, as said below
- segments: int32 [16384], P(('groups', 'seq')), parts along dimension 0, may hold values from 0 to 7, as said below
- context_grad: bfloat16 [16384, 768], P(('groups', 'seq')), parts along dimension 0, may hold values from -6 to 6
Outputs:
- context: bfloat16 [16384, 768], P(('groups', 'seq')), parts along dimension 0
- input_grad: bfloat16 [16384, 768], P(('groups', 'seq')), parts along dimension 0
- projection_grad: float32 [1536, 2304], P(('groups', 'seq')), parts along dimension 0
The draws below stay inside these ranges and needn't reach their ends.
There are 2 independent parts, one for each index of `groups`. The reference program is written for one: setup_inputs(seed, part) draws one part's arguments, and reference() takes and returns one part's arrays. A program takes and returns all parts, laid end to end along the dimension named above; an argument that names none is the same for every part. Nothing has to cross between parts.
Inputs may be any that keep to these rules, and one draw needn't show every extreme that they name: `segments`: segment ids never fall along the sequence; the first token has id 0, the last id 8 - 1, and every id in between occurs. positions are 0 at the first token of every segment; within a segment a position is the segment's time index capped at 1024, and the time index rises by 0 to 3 from one token to the next.
All inputs are finite; a program needn't handle non-finite values.
Results may differ from the reference program's by a relative error of at most 0.03.
The reference program's roundings to bfloat16 on the way (of `normed`, `values`, `probs`, `dscores` and `dqkv`) count: a program that leaves them out, or rounds other values in their place, can miss the bound.
Values may be sent and summed in bfloat16 or wider, within the bound.
A program may use at most 128 MiB of HBM per device.

```python
import math
import jax
import jax.numpy as jnp
from jax import lax

D = 768
H = 12
HD = 64
W = 1024
TOKENS = 8192
SEGS = 8


def segment_ids(key):
    cut_key = jax.random.fold_in(key, 11)
    cuts = jax.random.permutation(cut_key, TOKENS - W - 1)[:SEGS - 1].astype(jnp.int32) + W + 1
    places = jnp.arange(TOKENS, dtype=jnp.int32)
    return jnp.sum((places[:, None] >= cuts[None, :]).astype(jnp.int32), axis=1).astype(jnp.int32)


def tick_steps(key):
    loose = jax.random.randint(jax.random.fold_in(key, 12), (TOKENS,), 0, 4).astype(jnp.int32)
    firm = jax.random.randint(jax.random.fold_in(key, 13), (TOKENS,), 1, 4).astype(jnp.int32)
    places = jnp.arange(TOKENS, dtype=jnp.int32)
    return jnp.where(places <= W, firm, loose).astype(jnp.int32)


def draw_segments(key, part):
    return segment_ids(key)


def draw_positions(key, part):
    seg_ids = segment_ids(key)
    steps = tick_steps(key)
    before = (jnp.cumsum(steps) - steps).astype(jnp.int32)
    is_start = jnp.concatenate([jnp.ones((1,), jnp.bool_), seg_ids[1:] != seg_ids[:-1]])
    start_value = lax.cummax(jnp.where(is_start, before, 0), axis=0)
    return jnp.minimum(before - start_value, W).astype(jnp.int32)


def draw_inputs(key, part):
    base_key = jax.random.fold_in(key, 21)
    row_scale = jnp.exp(jax.random.uniform(jax.random.fold_in(key, 22), (TOKENS, 1), jnp.float32, 0.0, math.log(10.0)))
    col_scale = jnp.exp(jax.random.uniform(jax.random.fold_in(key, 23), (1, D), jnp.float32, 0.0, math.log(10.0)))
    base = jax.random.truncated_normal(base_key, -4.0, 4.0, (TOKENS, D), jnp.float32)
    return (base * row_scale * col_scale).astype(jnp.bfloat16)


def draw_projection(key, part):
    return (jax.random.truncated_normal(jax.random.fold_in(key, 33), -4.0, 4.0, (D, 3 * D), jnp.float32) / math.sqrt(D)).astype(jnp.bfloat16)


def block_levels(key, extent, shards, low, high):
    gain, own = 1.0, jax.random.fold_in(key, 6)
    for axis_at, blocks in shards:
        steps = jnp.exp(jax.random.uniform(jax.random.fold_in(own, axis_at), (blocks,), jnp.float32, low / len(shards), high / len(shards)))
        gain = gain * jnp.repeat(steps, extent[axis_at] // blocks).reshape([-1 if axis == axis_at else 1 for axis in range(len(extent))])
    return gain


def noise(stream_key, extent, width, bound, split=(), kind=jnp.bfloat16):
    entries = width * jax.random.normal(stream_key, extent, jnp.float32)
    if split:
        entries = entries * block_levels(stream_key, extent, split, -0.22, 0.18)
    return jnp.clip(entries, -bound, bound).astype(kind)


def setup_inputs(seed: int = 0, part: int = 0) -> dict:
    key_list = jax.random.split(jax.random.key(seed), 6)
    own_keys = jax.random.split(jax.random.fold_in(key_list[5], part), 6)
    return {
        "inputs": draw_inputs(jax.random.fold_in(jax.random.fold_in(key_list[5], part), 71), part),
        "projection": draw_projection(jax.random.fold_in(key_list[5], 71), part),
        "positions": draw_positions(jax.random.fold_in(jax.random.fold_in(key_list[5], part), 71), part),
        "segments": draw_segments(jax.random.fold_in(jax.random.fold_in(key_list[5], part), 71), part),
        "context_grad": noise(own_keys[4], (TOKENS, D), 1.0, 6.0, ((0, 16),)),
    }


EPSILON = 1e-05
SCORE_SCALE = 0.125
MASKED_SCORE = -1e+30

def rotary_tables(positions):
    half_size = HD // 2
    frequency = jnp.exp(-math.log(10000.0) * jnp.arange(half_size, dtype=jnp.float32) / half_size)
    angle = positions.astype(jnp.float32)[:, None] * frequency[None, :]
    return (jnp.cos(angle)[:, None, :], jnp.sin(angle)[:, None, :])

def rotate(tensor, cosine_table, sine_table):
    first_half = tensor[..., :HD // 2]
    second_half = tensor[..., HD // 2:]
    return jnp.concatenate([first_half * cosine_table - second_half * sine_table, second_half * cosine_table + first_half * sine_table], axis=-1)

def unrotate(tensor, cosine_table, sine_table):
    first_half = tensor[..., :HD // 2]
    second_half = tensor[..., HD // 2:]
    return jnp.concatenate([first_half * cosine_table + second_half * sine_table, second_half * cosine_table - first_half * sine_table], axis=-1)

def reference(inputs, projection, positions, segments, context_grad):
    x_float = inputs.astype(jnp.float32)
    inv_rms = lax.rsqrt(lax.optimization_barrier(jnp.mean(x_float * x_float, axis=1, keepdims=True)) + EPSILON)
    scaled = x_float * inv_rms
    normed = scaled.astype(jnp.bfloat16)
    projected = jnp.dot(normed, projection, preferred_element_type=jnp.float32)
    cosine_table, sine_table = rotary_tables(positions)
    q_rot = rotate(projected[:, :D].reshape(TOKENS, H, HD), cosine_table, sine_table).astype(jnp.bfloat16)
    k_rot = rotate(projected[:, D:2 * D].reshape(TOKENS, H, HD), cosine_table, sine_table).astype(jnp.bfloat16)
    values = projected[:, 2 * D:].reshape(TOKENS, H, HD).astype(jnp.bfloat16)
    out_grads = context_grad.reshape(TOKENS, H, HD)
    key_padded = jnp.concatenate([jnp.zeros((W, H, HD), jnp.bfloat16), k_rot], axis=0)
    value_padded = jnp.concatenate([jnp.zeros((W, H, HD), jnp.bfloat16), values], axis=0)
    seg_padded = jnp.concatenate([jnp.full((W,), -1, jnp.int32), segments.astype(jnp.int32)], axis=0)
    block_rows = min(256, TOKENS)
    block_count = TOKENS // block_rows
    key_span = block_rows + W
    offsets = jnp.arange(block_rows, dtype=jnp.int32)[:, None] + W - jnp.arange(key_span, dtype=jnp.int32)[None, :]

    def visit(carry, number):
        key_acc, value_acc = carry
        first_row = number * block_rows
        queries = lax.dynamic_slice_in_dim(q_rot, first_row, block_rows, 0)
        grad_rows = lax.dynamic_slice_in_dim(out_grads, first_row, block_rows, 0)
        query_seg = lax.dynamic_slice_in_dim(segments.astype(jnp.int32), first_row, block_rows, 0)
        key_block = lax.dynamic_slice_in_dim(key_padded, first_row, key_span, 0)
        value_block = lax.dynamic_slice_in_dim(value_padded, first_row, key_span, 0)
        key_seg = lax.dynamic_slice_in_dim(seg_padded, first_row, key_span, 0)
        allowed = (offsets >= 0) & (offsets < W) & (query_seg[:, None] == key_seg[None, :])
        scores = jnp.einsum('qhe,khe->hqk', queries.astype(jnp.float32), key_block.astype(jnp.float32)) * SCORE_SCALE
        masked = jnp.where(allowed[None], scores, MASKED_SCORE)
        row_max = lax.optimization_barrier(jnp.max(masked, axis=2, keepdims=True))
        log_total = row_max + jnp.log(lax.optimization_barrier(jnp.sum(jnp.exp(masked - row_max), axis=2, keepdims=True)))
        weights = jnp.exp(masked - log_total)
        probs = weights.astype(jnp.bfloat16)
        context = jnp.einsum('hqk,khe->qhe', probs.astype(jnp.float32), value_block.astype(jnp.float32)).astype(jnp.bfloat16)
        row_delta = lax.optimization_barrier(jnp.sum(grad_rows.astype(jnp.float32) * context.astype(jnp.float32), axis=2))
        dprobs = jnp.einsum('qhe,khe->hqk', grad_rows.astype(jnp.float32), value_block.astype(jnp.float32))
        dscores = (weights * (dprobs - jnp.transpose(row_delta)[:, :, None])).astype(jnp.bfloat16)
        query_grad = jnp.einsum('hqk,khe->qhe', dscores.astype(jnp.float32), key_block.astype(jnp.float32)) * SCORE_SCALE
        key_grad = jnp.einsum('hqk,qhe->khe', dscores.astype(jnp.float32), queries.astype(jnp.float32)) * SCORE_SCALE
        value_grad = jnp.einsum('hqk,qhe->khe', probs.astype(jnp.float32), grad_rows.astype(jnp.float32))
        key_acc = lax.dynamic_update_slice_in_dim(key_acc, lax.dynamic_slice_in_dim(key_acc, first_row, key_span, 0) + key_grad, first_row, 0)
        value_acc = lax.dynamic_update_slice_in_dim(value_acc, lax.dynamic_slice_in_dim(value_acc, first_row, key_span, 0) + value_grad, first_row, 0)
        return ((key_acc, value_acc), (context, query_grad))
    start_acc = (jnp.zeros((TOKENS + W, H, HD), jnp.float32), jnp.zeros((TOKENS + W, H, HD), jnp.float32))
    (key_acc, value_acc), (context_blocks, query_blocks) = lax.scan(visit, start_acc, jnp.arange(block_count, dtype=jnp.int32))
    context = context_blocks.reshape(TOKENS, D)
    query_grad = query_blocks.reshape(TOKENS, H, HD)
    query_lin = unrotate(query_grad, cosine_table, sine_table).reshape(TOKENS, D)
    key_lin = unrotate(key_acc[W:], cosine_table, sine_table).reshape(TOKENS, D)
    value_lin = value_acc[W:].reshape(TOKENS, D)
    dqkv = jnp.concatenate([query_lin, key_lin, value_lin], axis=1).astype(jnp.bfloat16)
    normed_grad = jnp.dot(dqkv, projection.T, preferred_element_type=jnp.float32)
    input_grad = (inv_rms * (normed_grad - scaled * lax.optimization_barrier(jnp.mean(normed_grad * scaled, axis=1, keepdims=True)))).astype(jnp.bfloat16)
    projection_grad = jnp.dot(normed.T, dqkv, preferred_element_type=jnp.float32) * TOKENS ** (-0.5)
    return (context, input_grad, projection_grad)
```

```python
import functools
import math

import jax
import jax.numpy as jnp
import numpy as np
from jax import lax
from jax.experimental import pallas as pl
from jax.experimental.pallas import tpu as pltpu
from jax.sharding import PartitionSpec as P

D = 768
H = 12
HD = 64
W = 1024
EPSILON = 1e-05
SCORE_SCALE = 0.125
MASKED_SCORE = -1e30
BLOCK = 256
SPAN = BLOCK + W
PAIR = 2 * HD
HALF = D // 2


def contract(a, b, da, db):
    return lax.dot_general(a, b, (((da,), (db,)), ((), ())), preferred_element_type=jnp.float32)


def swap_halves(u, lane):
    low = (lane % HD) < HD // 2
    return jnp.where(low, pltpu.roll(u, PAIR - HD // 2, 1), pltpu.roll(u, HD // 2, 1))


def pair_attention(
    p, nx_ref, wq_ref, wk_ref, wv_ref, cos_ref, sin_ref, segq_ref, segk_ref, do_ref,
    ctx_ref, dq_ref,
    bias, qs, ks, vs, dka, dva,
):
    own = ctx_ref.shape[0]
    total = nx_ref.shape[0]
    lane = lax.broadcasted_iota(jnp.int32, (1, PAIR), 1)

    def swap(u):
        return swap_halves(u, lane)

    @pl.when(p == 0)
    def _():
        row = lax.broadcasted_iota(jnp.int32, (BLOCK, SPAN), 0)
        col = lax.broadcasted_iota(jnp.int32, (BLOCK, SPAN), 1)
        near = (col > row) & (col <= row + W)
        for b in range(own // BLOCK):
            same = segq_ref[b * BLOCK : (b + 1) * BLOCK, :] == segk_ref[:, b * BLOCK : b * BLOCK + SPAN]
            bias[b] = jnp.where(near & same, 0.0, MASKED_SCORE)

    def project(i, carry):
        rows = pl.ds(pl.multiple_of(i * BLOCK, BLOCK), BLOCK)
        x = nx_ref[rows, :]
        k = contract(x, wk_ref[...], 1, 0)
        ks[rows, :] = (k * cos_ref[rows, :] + swap(k) * sin_ref[rows, :]).astype(jnp.bfloat16)
        vs[rows, :] = contract(x, wv_ref[...], 1, 0).astype(jnp.bfloat16)
        dka[rows, :] = jnp.zeros((BLOCK, PAIR), jnp.float32)
        dva[rows, :] = jnp.zeros((BLOCK, PAIR), jnp.float32)
        return carry

    lax.fori_loop(0, total // BLOCK, project, 0)

    def query(i, carry):
        rows = pl.ds(pl.multiple_of(i * BLOCK, BLOCK), BLOCK)
        here = pl.ds(pl.multiple_of(i * BLOCK + W, BLOCK), BLOCK)
        q = contract(nx_ref[here, :], wq_ref[...], 1, 0)
        q = (q * cos_ref[here, :] + swap(q) * sin_ref[here, :]).astype(jnp.bfloat16)
        qs[rows, :] = q * jnp.bfloat16(SCORE_SCALE)
        return carry

    lax.fori_loop(0, own // BLOCK, query, 0)

    def visit(b, carry):
        rows = pl.ds(pl.multiple_of(b * BLOCK, BLOCK), BLOCK)
        here = pl.ds(pl.multiple_of(b * BLOCK + W, BLOCK), BLOCK)
        window = pl.ds(pl.multiple_of(b * BLOCK, BLOCK), SPAN)
        contexts, grads = [], []
        for h in range(2):
            mine = (lane // HD) == h
            kb = ks[window, :]
            vb = vs[window, :]
            qh = jnp.where(mine, qs[rows, :], jnp.bfloat16(0))
            gh = jnp.where(mine, do_ref[rows, :], jnp.bfloat16(0))
            s = contract(qh, kb, 1, 1) + bias[b]
            e = jnp.exp(s - jnp.max(s, axis=1, keepdims=True))
            w = e * (1.0 / jnp.sum(e, axis=1, keepdims=True))
            pb = w.astype(jnp.bfloat16)
            context = contract(pb, vb, 1, 0).astype(jnp.bfloat16)
            delta = jnp.sum(
                gh.astype(jnp.float32) * context.astype(jnp.float32), axis=1, keepdims=True
            )
            dp = contract(gh, vb, 1, 1)
            ds = (w * (dp - delta)).astype(jnp.bfloat16)
            contexts.append(context)
            grads.append(contract(ds, kb, 1, 0))
            dka[window, :] += contract(ds, qh, 0, 0)
            dva[window, :] += contract(pb, gh, 0, 0)
        first = lane < HD
        ctx_ref[rows, :] = jnp.where(first, contexts[0], contexts[1])
        g = jnp.where(first, grads[0], grads[1]) * SCORE_SCALE
        dq_ref[rows, :] = (g * cos_ref[here, :] - swap(g) * sin_ref[here, :]).astype(jnp.bfloat16)
        return carry

    lax.fori_loop(0, own // BLOCK, visit, 0)


def attention_kernel(
    core_ref, nx_ref, wq_ref, wk_ref, wv_ref, cos_ref, sin_ref, segq_ref, segk_ref, do_ref,
    ctx_ref, dq_ref, dk_ref, dv_ref,
    bias, qs, ks, vs, dka, dva,
):
    total = nx_ref.shape[0]
    lane = lax.broadcasted_iota(jnp.int32, (1, PAIR), 1)

    def swap(u):
        return swap_halves(u, lane)

    pair_attention(
        pl.program_id(0), nx_ref, wq_ref, wk_ref, wv_ref, cos_ref, sin_ref, segq_ref, segk_ref,
        do_ref, ctx_ref, dq_ref, bias, qs, ks, vs, dka, dva,
    )

    def finish(i, carry):
        rows = pl.ds(pl.multiple_of(i * BLOCK, BLOCK), BLOCK)
        g = dka[rows, :]
        dk_ref[rows, :] = (g * cos_ref[rows, :] - swap(g) * sin_ref[rows, :]).astype(jnp.bfloat16)
        dv_ref[rows, :] = dva[rows, :].astype(jnp.bfloat16)
        return carry

    lax.fori_loop(0, total // BLOCK, finish, 0)


def attention(core, nx, weights, cosine, sine, seg_q, seg_k, out_grads):
    total = nx.shape[0]
    own = total - W
    pairs = HALF // PAIR

    def whole(shape):
        return pl.BlockSpec(shape, lambda p, c: (0, 0))

    def columns(start):
        return pl.BlockSpec((D, PAIR), lambda p, c: (0, start + c[0] * pairs + p))

    def heads(rows):
        return pl.BlockSpec((rows, PAIR), lambda p, c: (0, p))

    return pl.pallas_call(
        attention_kernel,
        out_shape=[
            jax.ShapeDtypeStruct((own, HALF), jnp.bfloat16),
            jax.ShapeDtypeStruct((own, HALF), jnp.bfloat16),
            jax.ShapeDtypeStruct((total, HALF), jnp.bfloat16),
            jax.ShapeDtypeStruct((total, HALF), jnp.bfloat16),
        ],
        grid_spec=pltpu.PrefetchScalarGridSpec(
            num_scalar_prefetch=1,
            grid=(pairs,),
            in_specs=[
                whole((total, D)),
                columns(0),
                columns(2 * pairs),
                columns(4 * pairs),
                whole((total, PAIR)),
                whole((total, PAIR)),
                whole((own, 1)),
                whole((1, total)),
                heads(own),
            ],
            out_specs=[heads(own), heads(own), heads(total), heads(total)],
            scratch_shapes=[
                pltpu.VMEM((own // BLOCK, BLOCK, SPAN), jnp.float32),
                pltpu.VMEM((own, PAIR), jnp.bfloat16),
                pltpu.VMEM((total, PAIR), jnp.bfloat16),
                pltpu.VMEM((total, PAIR), jnp.bfloat16),
                pltpu.VMEM((total, PAIR), jnp.float32),
                pltpu.VMEM((total, PAIR), jnp.float32),
            ],
        ),
        compiler_params=pltpu.CompilerParams(vmem_limit_bytes=48 * 1024 * 1024),
        name="window_attention",
    )(core, nx, weights, weights, weights, cosine, sine, seg_q, seg_k, out_grads)


ROWS = 512
HALVES = 2
TABLE = HD // 2


def turn(angle):
    count = jnp.floor(angle * (2.0 / math.pi) + 0.5)
    r = angle - count * 1.5703125
    r = r - count * 4.837512969970703125e-4
    r = r - count * 7.54978995489188e-8
    z = r * r
    s = r + r * z * (-1.6666654611e-1 + z * (8.3321608736e-3 - z * 1.9515295891e-4))
    c = 1.0 - 0.5 * z + z * z * (4.166664568298827e-2 + z * (-1.388731625493765e-3 + z * 2.443315711809948e-5))
    quarter = count - 4.0 * jnp.floor(count * 0.25)
    odd = (quarter == 1.0) | (quarter == 3.0)
    sine = jnp.where(odd, c, s)
    cosine = jnp.where(odd, s, c)
    sine = jnp.where(quarter >= 2.0, -sine, sine)
    cosine = jnp.where((quarter == 1.0) | (quarter == 2.0), -cosine, cosine)
    return cosine, sine


def rotated(u, c, s):
    parts = []
    for h in range(2):
        a = u[h * HD : h * HD + TABLE]
        b = u[h * HD + TABLE : (h + 1) * HD]
        parts += [a * c - b * s, b * c + a * s]
    return jnp.concatenate(parts, axis=0)


class Unit:
    pass


def attend(blocks, bias, qT, kT, vT, ks, vs, gT, ctxT, dqT, dkT, dvT):
    chunks = SPAN // BLOCK
    sub = lax.broadcasted_iota(jnp.int32, (PAIR, 1), 0)
    bf16, f32 = jnp.bfloat16, jnp.float32

    def unit(b, h):
        u = Unit()
        u.b, u.h = b, h
        u.cols = pl.ds(pl.multiple_of(b * BLOCK, BLOCK), BLOCK)
        u.head = slice(h * HD, (h + 1) * HD)
        u.mine = (sub // HD) == h
        return u

    def keys(u, c):
        return pl.ds(pl.multiple_of(u.b * BLOCK + c * BLOCK, BLOCK), BLOCK)

    def score(u, c):
        if c == 0:
            q = qT[:, u.cols]
            u.q, u.qh, u.s = jnp.where(u.mine, q, bf16(0)), q[u.head], []
        s = contract(ks[keys(u, c), :], u.q, 1, 0) + bias[u.b, c * BLOCK : (c + 1) * BLOCK, :]
        u.s.append(s)
        top = jnp.max(s.reshape(-1, 8, BLOCK), axis=0)
        u.m = top if c == 0 else jnp.maximum(u.m, top)
        if c == chunks - 1:
            u.m = jnp.max(u.m, axis=0, keepdims=True)

    def expand(u, c):
        if c == 0:
            u.e = []
        e = jnp.exp(u.s[c] - u.m)
        u.e.append(e)
        part = jnp.sum(e.reshape(-1, 8, BLOCK), axis=0)
        u.l = part if c == 0 else u.l + part
        if c == chunks - 1:
            u.inv = 1.0 / jnp.sum(u.l, axis=0, keepdims=True)

    def mix(u, c):
        if c == 0:
            u.w, u.p = [], []
        w = u.e[c] * u.inv
        u.w.append(w)
        u.p.append(w.astype(bf16))
        t = contract(vT[u.head, keys(u, c)], u.p[c], 1, 0)
        u.ctx = t if c == 0 else u.ctx + t
        if c == chunks - 1:
            g = gT(u.cols)
            u.g, u.gh = jnp.where(u.mine, g, bf16(0)), g[u.head]
            u.ctx = u.ctx.astype(bf16)
            ctxT[u.head, u.cols] = u.ctx
            u.delta = jnp.sum(u.gh.astype(f32) * u.ctx.astype(f32), axis=0, keepdims=True)

    def slope(u, c):
        if c == 0:
            u.ds = []
        dp = contract(vs[keys(u, c), :], u.g, 1, 0)
        u.ds.append((u.w[c] * (dp - u.delta)).astype(bf16))
        dvT[u.head, keys(u, c)] += contract(u.gh, u.p[c], 1, 1)

    def back(u, c):
        t = contract(kT[u.head, keys(u, c)], u.ds[c], 1, 0)
        u.dq = t if c == 0 else u.dq + t
        dkT[u.head, keys(u, c)] += contract(u.qh, u.ds[c], 1, 1)
        if c == chunks - 1:
            dqT[u.head, u.cols] = u.dq

    stages = [score, expand, mix, slope, back]
    units = [unit(b, h) for b in blocks for h in range(2)]
    for t in range(len(stages) + len(units) - 1):
        for c in range(chunks):
            for n, u in enumerate(units):
                if 0 <= t - n < len(stages):
                    stages[t - n](u, c)


def whole_kernel(
    x_ref, w_ref, pos_ref, seg_ref, g_ref, freq_ref,
    ctx_ref, ig_ref, pg_ref,
    nx, rms, wg, wpack, wT, meta, metag, gsend, gbuf, gT, cosT, sinT, segc, bias,
    qT, kT, vT, ks, vs, ctxT, dqT, dkT, dvT, dqb, dkvb, dtok,
    ctxs, ctxr, part, sums, ps, pr, fwd, later, ys, yr, ngo,
    w_send, w_recv, x_send, x_recv, m_send, m_recv, g_send, g_recv,
    part_send, part_recv, ctx_send, ctx_recv, n_send, n_recv,
    *, count, grad_scale,
):
    f32, bf16 = jnp.float32, jnp.bfloat16
    me = lax.axis_index("seq")
    core = lax.rem(me, 2)
    chip = lax.div(me, 2)
    chips = count // 2
    layers = count // 4
    partner = me + 1 - 2 * core
    side = lax.rem(chip, 2)
    layer = lax.div(chip, 2)
    across = me + 2 - 4 * side
    share = D // count
    total = 2 * W
    mine_at = pl.multiple_of(core * ROWS, ROWS)
    other_at = pl.multiple_of((1 - core) * ROWS, ROWS)
    has_prev = chip > 0
    has_next = chip < chips - 1
    prev = lax.rem(me + count - 2, count)
    after = lax.rem(me + 2, count)

    def remote(source, target, send, recv, device):
        return pltpu.make_async_remote_copy(
            src_ref=source, dst_ref=target, send_sem=send, recv_sem=recv,
            device_id={"seq": device}, device_id_type=pl.DeviceIdType.MESH,
        )

    barrier = pltpu.get_barrier_semaphore()

    def greet(i, carry):
        pl.semaphore_signal(
            barrier, inc=1, device_id={"seq": lax.rem(me + 1 + i, count)},
            device_id_type=pl.DeviceIdType.MESH,
        )
        return carry

    lax.fori_loop(0, count - 1, greet, 0)

    for p in range(3):
        for h in range(2):
            wpack[p, h] = jnp.concatenate(
                [w_ref[:, t * D + h * HALF + p * PAIR : t * D + h * HALF + (p + 1) * PAIR] for t in range(3)],
                axis=1,
            )

    meta[0:1, :] = pos_ref[...]
    meta[1:2, :] = seg_ref[...]
    metag[2 + core] = meta[...]

    own_block = pl.ds(pl.multiple_of(me * share, share), share)
    for p in range(3):
        wg[p, own_block, :] = wpack[p, core]

    def block_of(device):
        return pl.ds(pl.multiple_of(device * share, share), share)

    def w_own(p, j):
        hop = lax.div(j + 1, 2)
        turn_core = lax.rem(j + 1, 2)
        far = lax.rem(layer + hop, layers)
        to = lax.rem(core + turn_core, 2)
        device = (far * 2 + side) * 2 + to
        return remote(
            wpack.at[p, to], wg.at[p, own_block, :],
            w_send.at[p, j], w_recv.at[p, layer * 2 + core], device,
        )

    def w_from(p, j):
        hop = lax.div(j + 1, 2)
        turn_core = lax.rem(j + 1, 2)
        near = lax.rem(layer + layers - hop, layers)
        source_core = lax.rem(core + turn_core, 2)
        device = (near * 2 + side) * 2 + source_core
        return device, near * 2 + source_core

    def w_arrival(p, j):
        device, slot = w_from(p, j)
        return remote(
            wpack.at[p, 0], wg.at[p, block_of(device), :], w_send.at[p, j], w_recv.at[p, slot], device
        )

    planes = 2 * layers - 1

    def w_across_own(p):
        return remote(
            wg.at[p, own_block, :], wg.at[p, own_block, :],
            w_send.at[p, planes], w_recv.at[p, 2 * layers + layer * 2 + core], across,
        )

    def w_across(p, j):
        device, slot = w_from(p, j)
        return remote(
            wg.at[p, block_of(device), :], wg.at[p, block_of(device), :],
            w_send.at[p, planes + 1 + j], w_recv.at[p, 2 * layers + slot], across,
        )

    def w_across_arrival(p, s):
        device = (lax.div(s, 2) * 2 + (1 - side)) * 2 + lax.rem(s, 2)
        return remote(
            wg.at[p, block_of(device), :], wg.at[p, block_of(device), :],
            w_send.at[p, planes], w_recv.at[p, 2 * layers + s], across,
        )

    def loop(n, body):
        def step(i, carry):
            body(i)
            return carry

        lax.fori_loop(0, n, step, 0)

    def send_weights(p):
        w_across_own(p).start()
        loop(planes, lambda j: w_own(p, j).start())

    def relay_weights(p):
        def step(j):
            w_arrival(p, j).wait_recv()
            w_across(p, j).start()

        loop(planes, step)

    def await_weights(p):
        loop(2 * layers, lambda s: w_across_arrival(p, s).wait_recv())

    mine_rows = pl.ds(pl.multiple_of(W + mine_at, ROWS), ROWS)
    other_rows = pl.ds(pl.multiple_of(W + other_at, ROWS), ROWS)

    def chunk_rows(base, k):
        return pl.ds(pl.multiple_of(base + k * BLOCK, BLOCK), BLOCK)

    def x_swap():
        return remote(nx.at[mine_rows], nx.at[mine_rows], x_send.at[0], x_recv.at[0], partner)

    def x_swap_arrival():
        return remote(nx.at[other_rows], nx.at[other_rows], x_send.at[0], x_recv.at[0], partner)

    def x_next(k):
        return remote(
            nx.at[chunk_rows(W + mine_at, k)], nx.at[chunk_rows(mine_at, k)],
            x_send.at[1 + k], x_recv.at[1 + k], after,
        )

    def x_relay(k):
        return remote(
            nx.at[chunk_rows(mine_at, k)], nx.at[chunk_rows(mine_at, k)],
            x_send.at[3 + k], x_recv.at[3 + k], partner,
        )

    def x_relay_arrival(k):
        return remote(
            nx.at[chunk_rows(other_at, k)], nx.at[chunk_rows(other_at, k)],
            x_send.at[3 + k], x_recv.at[3 + k], partner,
        )

    def m_swap():
        return remote(metag.at[2 + core], metag.at[2 + core], m_send.at[0], m_recv.at[0], partner)

    def m_swap_arrival():
        return remote(metag.at[3 - core], metag.at[3 - core], m_send.at[0], m_recv.at[0], partner)

    def m_next(t):
        device = after - core + t
        return remote(meta, metag.at[core], m_send.at[1 + t], m_recv.at[1 + core], device)

    def m_prev_arrival(t):
        return remote(meta, metag.at[t], m_send.at[1 + t], m_recv.at[1 + t], prev)

    def g_swap():
        return remote(gsend, gbuf.at[pl.ds(mine_at, ROWS), :], g_send, g_recv, partner)

    def g_arrival():
        return remote(gsend, gbuf.at[pl.ds(other_at, ROWS), :], g_send, g_recv, partner)

    half_mine = pl.ds(pl.multiple_of(core * HALF, HALF), HALF)
    half_other = pl.ds(pl.multiple_of((1 - core) * HALF, HALF), HALF)
    gsend[...] = g_ref[:, half_other]
    gbuf[pl.ds(mine_at, ROWS), :] = g_ref[:, half_mine]

    def normalize(k):
        rows = pl.ds(pl.multiple_of(k * BLOCK, BLOCK), BLOCK)
        x = x_ref[rows, :].astype(f32)
        inv = lax.rsqrt(jnp.mean(x * x, axis=1, keepdims=True) + EPSILON)
        rms[rows, :] = inv
        nx[chunk_rows(W + mine_at, k), :] = (x * inv).astype(bf16)

    loop(2, normalize)

    pl.semaphore_wait(barrier, count - 1)
    send_weights(0)
    m_swap().start()
    x_swap().start()
    g_swap().start()

    @pl.when(has_next)
    def _():
        m_next(0).start()
        m_next(1).start()
        x_next(1).start()
        x_next(0).start()

    relay_weights(0)
    send_weights(1)
    send_weights(2)

    @pl.when(has_prev)
    def _():
        m_prev_arrival(0).wait_recv()
        m_prev_arrival(1).wait_recv()

    @pl.when(jnp.logical_not(has_prev))
    def _():
        row = lax.broadcasted_iota(jnp.int32, (8, ROWS), 0)
        gone = jnp.where(row == 1, -1, 0)
        metag[0] = gone
        metag[1] = gone
        nx[:W, :] = jnp.zeros((W, D), bf16)

    m_swap_arrival().wait_recv()
    g_arrival().wait_recv()

    for n in range(4):
        angle = metag[n][0:1, :].astype(f32) * freq_ref[:, 0:1]
        c, s = turn(angle)
        cosT[:, n * ROWS : (n + 1) * ROWS] = c
        sinT[:, n * ROWS : (n + 1) * ROWS] = s
        seg = metag[n][1:2, :].astype(f32)
        for j in range(ROWS // PAIR):
            flat = jnp.broadcast_to(seg[:, j * PAIR : (j + 1) * PAIR], (PAIR, PAIR))
            segc[n * ROWS + j * PAIR : n * ROWS + (j + 1) * PAIR, :] = jnp.transpose(flat)
    for n in range(2):
        gT[:, n * ROWS : (n + 1) * ROWS] = jnp.transpose(gbuf[n * ROWS : (n + 1) * ROWS, :])

    key = lax.broadcasted_iota(jnp.int32, (BLOCK, BLOCK), 0)
    query = lax.broadcasted_iota(jnp.int32, (BLOCK, BLOCK), 1)
    for b in range(W // BLOCK):
        at = b * BLOCK
        seg_q = metag[2 + at // ROWS][1:2, at % ROWS : at % ROWS + BLOCK].astype(f32)
        for c in range(SPAN // BLOCK):
            seg_k = segc[at + c * BLOCK : at + (c + 1) * BLOCK, :]
            same = jnp.concatenate([seg_k == seg_q[:, :PAIR], seg_k == seg_q[:, PAIR:]], axis=1)
            if c == 0:
                same = same & (key > query)
            if c == SPAN // BLOCK - 1:
                same = same & (key <= query)
            bias[b, c * BLOCK : (c + 1) * BLOCK, :] = jnp.where(same, 0.0, MASKED_SCORE)

    def table(n):
        cols = pl.ds(pl.multiple_of(n * BLOCK, BLOCK), BLOCK)
        return cols, cosT[:, cols], sinT[:, cols]

    def project_before(n):
        cols, c, s = table(n)
        kv = contract(wT[PAIR:, :], nx[cols, :], 1, 1)
        k = rotated(kv[:PAIR], c, s).astype(bf16)
        v = kv[PAIR:].astype(bf16)
        kT[:, cols] = k
        vT[:, cols] = v
        ks[cols, :] = jnp.transpose(k)
        vs[cols, :] = jnp.transpose(v)

    def project_own(i):
        n = i + W // BLOCK
        cols, c, s = table(n)
        at = pl.ds(pl.multiple_of(i * BLOCK, BLOCK), BLOCK)
        qkv = contract(wT[...], nx[cols, :], 1, 1)
        qT[:, at] = rotated(qkv[:PAIR], c, s).astype(bf16) * bf16(SCORE_SCALE)
        k = rotated(qkv[PAIR : 2 * PAIR], c, s).astype(bf16)
        v = qkv[2 * PAIR :].astype(bf16)
        kT[:, cols] = k
        vT[:, cols] = v
        ks[cols, :] = jnp.transpose(k)
        vs[cols, :] = jnp.transpose(v)

    def finish_chunk(p, n):
        cols, c, s = table(n)
        k = rotated(dkT[:, cols], c, -s).astype(bf16)
        v = dvT[:, cols].astype(bf16)
        kv = jnp.concatenate([k, v], axis=0)
        dkvb[:, cols] = kv
        dtok[p, cols, PAIR:] = jnp.transpose(kv)

    def finish_query(p, i):
        cols, c, s = table(i + W // BLOCK)
        at = pl.ds(pl.multiple_of(i * BLOCK, BLOCK), BLOCK)
        q = rotated(dqT[:, at] * SCORE_SCALE, c, -s).astype(bf16)
        dqb[:, at] = q
        dtok[p, cols, :PAIR] = jnp.transpose(q)
        ctxs[p, at, :] = jnp.transpose(ctxT[:, at])

    def ctx_copy(p):
        return remote(
            ctxs.at[p, pl.ds(other_at, ROWS), :], ctxr.at[p], ctx_send.at[p], ctx_recv.at[p], partner
        )

    def part_copy(p, i):
        target = lax.rem(me + 1 + i, count)
        return remote(
            part.at[p, block_of(target), :], sums.at[p, i],
            part_send.at[p, i], part_recv.at[p, i], target,
        )

    def n_swap(k):
        return remote(ps.at[k], pr.at[k], n_send.at[k], n_recv.at[k], partner)

    def n_back(k):
        return remote(fwd.at[k], later.at[k], n_send.at[2 + k], n_recv.at[2 + k], prev)

    def n_own():
        return remote(ys, yr, n_send.at[4], n_recv.at[4], partner)

    def before_grad(half, k):
        rows = chunk_rows(half * ROWS, k)
        return sum(
            contract(dtok[p, rows, PAIR:], wg[p, :, PAIR:], 1, 1) for p in range(3)
        )

    def give_before(half):
        owner = core == half

        def step(k):
            mine = before_grad(half, k)

            @pl.when(jnp.logical_not(owner))
            def _():
                ps[k] = mine.astype(bf16)
                n_swap(k).start()

            @pl.when(owner)
            def _():
                ngo[pl.ds(pl.multiple_of(k * BLOCK, BLOCK), BLOCK), :] = mine

        loop(2, step)

    def pass_before(half):
        @pl.when(core == half)
        def _():
            for k in range(2):
                n_swap(k).wait_recv()
                fwd[k] = (ngo[k * BLOCK : (k + 1) * BLOCK, :] + pr[k].astype(f32)).astype(bf16)

                @pl.when(has_prev)
                def _():
                    n_back(k).start()

    def own_grad(at, k):
        rows = chunk_rows(W + at, k)
        return sum(contract(dtok[p, rows, :], wg[p], 1, 1) for p in range(3))

    def step(t):
        p = lax.div(t, 2)
        i = lax.rem(t, 2)
        half = jnp.where(p == 0, 1 - i, i)

        @pl.when(i == 0)
        def _():
            await_weights(p)
            wT[...] = jnp.transpose(wg[p])

            @pl.when(p == 0)
            def _():
                x_swap_arrival().wait_recv()

            loop(4, project_own)

            @pl.when(p > 0)
            def _():
                loop(4, project_before)

            dkT[...] = jnp.zeros_like(dkT)
            dvT[...] = jnp.zeros_like(dvT)

        @pl.when(p == 0)
        def _():
            @pl.when(has_prev)
            def _():
                @pl.when(core == half)
                def _():
                    for k in (1, 0):
                        x_next(k).wait_recv()
                        x_relay(k).start()

                @pl.when(core != half)
                def _():
                    for k in (1, 0):
                        x_relay_arrival(k).wait_recv()

            loop(2, lambda k: project_before(half * 2 + k))

        attend(
            [half * 2, half * 2 + 1], bias, qT, kT, vT, ks, vs,
            lambda cols: gT[pl.ds(pl.multiple_of(p * PAIR, PAIR), PAIR), cols],
            ctxT, dqT, dkT, dvT,
        )

        @pl.when(t < 2)
        def _():
            relay_weights(t + 1)

        @pl.when(t == 4)
        def _():
            loop(2, lambda n: finish_chunk(p, n))
            give_before(0)

        @pl.when(i == 1)
        def _():
            @pl.when(p == 2)
            def _():
                pass_before(0)

            loop(4, lambda n: finish_query(p, n))
            ctx_copy(p).start()

            @pl.when(p < 2)
            def _():
                loop(2, lambda n: finish_chunk(p, n))

            loop(6, lambda n: finish_chunk(p, n + 2))

            @pl.when(p == 2)
            def _():
                give_before(1)

            kv = contract(dkvb[...], nx[...], 1, 0)
            q = contract(dqb[...], nx[W:, :], 1, 0)
            part[p, :, :PAIR] = jnp.transpose(q.astype(bf16))
            part[p, :, PAIR:] = jnp.transpose(kv.astype(bf16))
            loop(count - 1, lambda j: part_copy(p, j).start())

    loop(6, step)

    pass_before(1)

    def give_own(k):
        ys[pl.ds(pl.multiple_of(k * BLOCK, BLOCK), BLOCK), :] = own_grad(other_at, k).astype(bf16)

    loop(2, give_own)
    n_own().start()

    def keep_own(k):
        ngo[pl.ds(pl.multiple_of(k * BLOCK, BLOCK), BLOCK), :] = own_grad(mine_at, k)

    loop(2, keep_own)

    for p in range(3):
        ctx_copy(p).wait()
        mine_cols = pl.ds(pl.multiple_of(core * HALF + p * PAIR, PAIR), PAIR)
        other_cols = pl.ds(pl.multiple_of((1 - core) * HALF + p * PAIR, PAIR), PAIR)
        ctx_ref[:, mine_cols] = ctxs[p, pl.ds(mine_at, ROWS), :]
        ctx_ref[:, other_cols] = ctxr[p]

    def sum_pair(p):
        loop(count - 1, lambda i: part_copy(p, i).wait())

        def add(i, carry):
            odd, even = carry
            return (odd + sums[p, 2 * i].astype(f32), even + sums[p, 2 * i + 1].astype(f32))

        kept = part[p, own_block, :]
        odd, even = lax.fori_loop(
            0, count // 2 - 1, add, (jnp.zeros((share, 3 * PAIR), f32), kept.astype(f32))
        )
        odd = odd + sums[p, count - 2].astype(f32)
        for t in range(3):
            at = t * D + p * PAIR
            a = pl.ds(pl.multiple_of(at + core * HALF, PAIR), PAIR)
            b = pl.ds(pl.multiple_of(at + (1 - core) * HALF, PAIR), PAIR)
            pg_ref[:, a] = even[:, t * PAIR : (t + 1) * PAIR] * grad_scale
            pg_ref[:, b] = odd[:, t * PAIR : (t + 1) * PAIR] * grad_scale

    sum_pair(0)
    sum_pair(1)
    n_own().wait()

    @pl.when(has_next)
    def _():
        n_back(0).wait_recv()
        n_back(1).wait_recv()

    @pl.when(jnp.logical_not(has_next))
    def _():
        later[...] = jnp.zeros_like(later)

    def finish(k):
        rows = pl.ds(pl.multiple_of(k * BLOCK, BLOCK), BLOCK)
        ng = ngo[rows, :] + yr[rows, :].astype(f32) + later[k].astype(f32)
        inv = rms[rows, :]
        scaled = x_ref[rows, :].astype(f32) * inv
        ig_ref[rows, :] = (
            inv * (ng - scaled * jnp.mean(ng * scaled, axis=1, keepdims=True))
        ).astype(bf16)

    loop(2, finish)
    sum_pair(2)

    for p in range(3):
        w_across_own(p).wait_send()

        def sent(j):
            w_own(p, j).wait_send()
            w_across(p, j).wait_send()

        loop(planes, sent)
    m_swap().wait_send()
    x_swap().wait_send()
    g_swap().wait_send()

    @pl.when(has_next)
    def _():
        for k in range(2):
            m_next(k).wait_send()
            x_next(k).wait_send()

    @pl.when(has_prev)
    def _():
        for k in range(2):
            x_relay(k).wait_send()
            n_back(k).wait_send()

    for k in range(2):
        n_swap(k).wait_send()


def whole(count, grad_scale, x, weights, positions, segments, out_grads):
    share = D // count
    bf16, f32 = jnp.bfloat16, jnp.float32
    total = 2 * W
    vmem = pl.BlockSpec(memory_space=pltpu.VMEM)
    frequency = np.exp(np.float32(-math.log(10000.0)) * np.arange(TABLE, dtype=np.float32) / np.float32(TABLE))
    frequency = np.broadcast_to(frequency.astype(np.float32)[:, None], (TABLE, PAIR))
    dma = pltpu.SemaphoreType.DMA
    planes = count // 2 - 1
    return pl.pallas_call(
        functools.partial(whole_kernel, count=count, grad_scale=grad_scale),
        out_shape=[
            jax.ShapeDtypeStruct((ROWS, D), bf16),
            jax.ShapeDtypeStruct((ROWS, D), bf16),
            jax.ShapeDtypeStruct((share, 3 * D), f32),
        ],
        in_specs=[vmem] * 6,
        out_specs=[vmem] * 3,
        scratch_shapes=[
            pltpu.VMEM((total, D), bf16),
            pltpu.VMEM((ROWS, 1), f32),
            pltpu.VMEM((3, D, 3 * PAIR), bf16),
            pltpu.VMEM((3, 2, share, 3 * PAIR), bf16),
            pltpu.VMEM((3 * PAIR, D), bf16),
            pltpu.VMEM((8, ROWS), jnp.int32),
            pltpu.VMEM((4, 8, ROWS), jnp.int32),
            pltpu.VMEM((ROWS, HALF), bf16),
            pltpu.VMEM((W, HALF), bf16),
            pltpu.VMEM((HALF, W), bf16),
            pltpu.VMEM((TABLE, total), f32),
            pltpu.VMEM((TABLE, total), f32),
            pltpu.VMEM((total, PAIR), f32),
            pltpu.VMEM((W // BLOCK, SPAN, BLOCK), f32),
            pltpu.VMEM((PAIR, W), bf16),
            pltpu.VMEM((PAIR, total), bf16),
            pltpu.VMEM((PAIR, total), bf16),
            pltpu.VMEM((total, PAIR), bf16),
            pltpu.VMEM((total, PAIR), bf16),
            pltpu.VMEM((PAIR, W), bf16),
            pltpu.VMEM((PAIR, W), f32),
            pltpu.VMEM((PAIR, total), f32),
            pltpu.VMEM((PAIR, total), f32),
            pltpu.VMEM((PAIR, W), bf16),
            pltpu.VMEM((2 * PAIR, total), bf16),
            pltpu.VMEM((3, total, 3 * PAIR), bf16),
            pltpu.VMEM((3, W, PAIR), bf16),
            pltpu.VMEM((3, ROWS, PAIR), bf16),
            pltpu.VMEM((3, D, 3 * PAIR), bf16),
            pltpu.VMEM((3, count - 1, share, 3 * PAIR), bf16),
            pltpu.VMEM((2, BLOCK, D), bf16),
            pltpu.VMEM((2, BLOCK, D), bf16),
            pltpu.VMEM((2, BLOCK, D), bf16),
            pltpu.VMEM((2, BLOCK, D), bf16),
            pltpu.VMEM((ROWS, D), bf16),
            pltpu.VMEM((ROWS, D), bf16),
            pltpu.VMEM((ROWS, D), f32),
            dma((3, 2 * planes + 1)), dma((3, 2 * planes + 2)),
            dma((5,)), dma((5,)),
            dma((3,)), dma((3,)),
            dma, dma,
            dma((3, count - 1)), dma((3, count - 1)),
            dma((3,)), dma((3,)),
            dma((5,)), dma((5,)),
        ],
        compiler_params=pltpu.CompilerParams(
            vmem_limit_bytes=60 * 1024 * 1024, collective_id=0, has_side_effects=True
        ),
        name="whole_sublayer",
    )(x, weights, positions, segments, out_grads, frequency)


def swapped(value):
    count = lax.axis_size("seq")
    return lax.ppermute(value, "seq", [(s, s ^ 1) for s in range(count)])


def chip_shifted(value, steps):
    count = lax.axis_size("seq")
    pairs = [(s, s + 2 * steps) for s in range(count) if 0 <= s + 2 * steps < count]
    return lax.ppermute(value, "seq", pairs)


def ordered(core, mine, other, axis=0):
    first = jnp.where(core == 0, mine, other)
    second = jnp.where(core == 0, other, mine)
    return jnp.concatenate([first, second], axis=axis)


def local(inputs, projection, positions, segments, context_grad):
    row_count = inputs.shape[0]
    device_count = lax.axis_size("seq")
    chips = device_count // 2
    device_index = lax.axis_index("seq")
    core = device_index % 2
    chip = device_index // 2
    assert 2 * row_count == W
    grad_scale = (row_count * device_count) ** (-0.5)

    if (D // device_count) % 16 == 0:
        return tuple(
            whole(
                device_count, grad_scale, inputs, projection, positions[None, :], segments[None, :],
                context_grad,
            )
        )

    weights = lax.all_gather(projection, "seq", axis=0, tiled=True)

    meta = jnp.stack([positions, segments], axis=0)
    x_before = chip_shifted(inputs, 1)
    meta_before = chip_shifted(meta, 1)
    x_other = swapped(inputs)
    meta_other = swapped(meta)
    x_before_other = swapped(x_before)
    meta_before_other = swapped(meta_before)
    grad_mine = lax.dynamic_slice_in_dim(context_grad, core * HALF, HALF, 1)
    grad_sent = lax.dynamic_slice_in_dim(context_grad, (1 - core) * HALF, HALF, 1)
    grad_other = swapped(grad_sent)
    out_grads = ordered(core, grad_mine, grad_other)

    x_all = jnp.concatenate(
        [ordered(core, x_before, x_before_other), ordered(core, inputs, x_other)], axis=0
    ).astype(jnp.float32)
    nx = (
        x_all * lax.rsqrt(jnp.mean(x_all * x_all, axis=1, keepdims=True) + EPSILON)
    ).astype(jnp.bfloat16)
    meta_all = jnp.concatenate(
        [ordered(core, meta_before, meta_before_other, 1), ordered(core, meta, meta_other, 1)],
        axis=1,
    )
    half_size = HD // 2
    frequency = jnp.exp(-math.log(10000.0) * jnp.arange(half_size, dtype=jnp.float32) / half_size)
    angle = meta_all[0].astype(jnp.float32)[:, None] * frequency[None, :]
    c, s = jnp.cos(angle), jnp.sin(angle)
    cosine = jnp.concatenate([c, c, c, c], axis=1)
    sine = jnp.concatenate([-s, s, -s, s], axis=1)
    seg_all = meta_all[1]
    outside = (jnp.arange(seg_all.shape[0]) < W) & (chip == 0)
    seg_k = jnp.where(outside, -1, seg_all)[None, :]
    seg_q = seg_all[W:][:, None]

    x_float = inputs.astype(jnp.float32)
    inv_rms = lax.rsqrt(jnp.mean(x_float * x_float, axis=1, keepdims=True) + EPSILON)
    scaled = x_float * inv_rms

    context_heads, dq, dk, dv = attention(
        core.astype(jnp.int32)[None], nx, weights, cosine, sine, seg_q, seg_k, out_grads
    )

    mine_at = core * row_count
    other_at = (1 - core) * row_count
    context_mine = lax.dynamic_slice_in_dim(context_heads, mine_at, row_count, 0)
    context_other = swapped(lax.dynamic_slice_in_dim(context_heads, other_at, row_count, 0))
    context = ordered(core, context_mine, context_other, 1)

    w_q, w_k, w_v = [
        lax.dynamic_slice_in_dim(weights, t * D + core * HALF, HALF, 1) for t in range(3)
    ]
    dkv = jnp.concatenate([dk, dv], axis=1)
    w_kv = jnp.concatenate([w_k, w_v], axis=1)
    ng_kv = contract(dkv, w_kv, 1, 1)
    ng_q = contract(dq, w_q, 1, 1)
    ng_before = ng_kv[:W]
    ng_own = ng_kv[W:] + ng_q
    send_before = lax.dynamic_slice_in_dim(ng_before, other_at, row_count, 0).astype(jnp.bfloat16)
    keep_before = lax.dynamic_slice_in_dim(ng_before, mine_at, row_count, 0)
    before = keep_before + swapped(send_before).astype(jnp.float32)
    later = chip_shifted(before.astype(jnp.bfloat16), -1)
    send_own = lax.dynamic_slice_in_dim(ng_own, other_at, row_count, 0).astype(jnp.bfloat16)
    keep_own = lax.dynamic_slice_in_dim(ng_own, mine_at, row_count, 0)
    normed_grad = (
        keep_own + swapped(send_own).astype(jnp.float32) + later.astype(jnp.float32)
    )
    input_grad = (
        inv_rms * (normed_grad - scaled * jnp.mean(normed_grad * scaled, axis=1, keepdims=True))
    ).astype(jnp.bfloat16)

    pg_kv = contract(nx, dkv, 0, 0)
    pg_q = contract(nx[W:], dq, 0, 0)
    pg = jnp.concatenate([pg_q, pg_kv], axis=1).astype(jnp.bfloat16)
    groups = [[2 * i + k for i in range(chips)] for k in range(2)]
    summed = lax.psum_scatter(
        pg, "seq", scatter_dimension=0, axis_index_groups=groups, tiled=True
    ).astype(jnp.float32)
    rows = summed.shape[0] // 2
    keep = lax.dynamic_slice_in_dim(summed, core * rows, rows, 0)
    other = swapped(lax.dynamic_slice_in_dim(summed, (1 - core) * rows, rows, 0).astype(jnp.bfloat16))
    other = other.astype(jnp.float32)
    parts = []
    for t in range(3):
        cols = slice(t * HALF, (t + 1) * HALF)
        parts.append(ordered(core, keep[:, cols], other[:, cols], 1))
    projection_grad = jnp.concatenate(parts, axis=1) * grad_scale
    return (context, input_grad, projection_grad)


def solution(mesh):
    in_specs = (
        P(("groups", "seq"), None),
        P("seq", None),
        P(("groups", "seq")),
        P(("groups", "seq")),
        P(("groups", "seq"), None),
    )
    out_specs = (P(("groups", "seq"), None), P(("groups", "seq"), None), P(("groups", "seq"), None))
    return jax.shard_map(local, mesh=mesh, in_specs=in_specs, out_specs=out_specs, check_vma=False)
```

```python
import functools
import math

import jax
import jax.numpy as jnp
import numpy as np
from jax import lax
from jax.experimental import pallas as pl
from jax.experimental.pallas import tpu as pltpu
from jax.sharding import PartitionSpec as P

D = 768
H = 12
HD = 64
W = 1024
EPSILON = 1e-05
SCORE_SCALE = 0.125
MASKED_SCORE = -1e30
BLOCK = 256
SPAN = BLOCK + W
PAIR = 2 * HD
HALF = D // 2


def contract(a, b, da, db):
    return lax.dot_general(a, b, (((da,), (db,)), ((), ())), preferred_element_type=jnp.float32)


def swap_halves(u, lane):
    low = (lane % HD) < HD // 2
    return jnp.where(low, pltpu.roll(u, PAIR - HD // 2, 1), pltpu.roll(u, HD // 2, 1))


def pair_attention(
    p, nx_ref, wq_ref, wk_ref, wv_ref, cos_ref, sin_ref, segq_ref, segk_ref, do_ref,
    ctx_ref, dq_ref,
    bias, qs, ks, vs, dka, dva,
):
    own = ctx_ref.shape[0]
    total = nx_ref.shape[0]
    lane = lax.broadcasted_iota(jnp.int32, (1, PAIR), 1)

    def swap(u):
        return swap_halves(u, lane)

    @pl.when(p == 0)
    def _():
        row = lax.broadcasted_iota(jnp.int32, (BLOCK, SPAN), 0)
        col = lax.broadcasted_iota(jnp.int32, (BLOCK, SPAN), 1)
        near = (col > row) & (col <= row + W)
        for b in range(own // BLOCK):
            same = segq_ref[b * BLOCK : (b + 1) * BLOCK, :] == segk_ref[:, b * BLOCK : b * BLOCK + SPAN]
            bias[b] = jnp.where(near & same, 0.0, MASKED_SCORE)

    def project(i, carry):
        rows = pl.ds(pl.multiple_of(i * BLOCK, BLOCK), BLOCK)
        x = nx_ref[rows, :]
        k = contract(x, wk_ref[...], 1, 0)
        ks[rows, :] = (k * cos_ref[rows, :] + swap(k) * sin_ref[rows, :]).astype(jnp.bfloat16)
        vs[rows, :] = contract(x, wv_ref[...], 1, 0).astype(jnp.bfloat16)
        dka[rows, :] = jnp.zeros((BLOCK, PAIR), jnp.float32)
        dva[rows, :] = jnp.zeros((BLOCK, PAIR), jnp.float32)
        return carry

    lax.fori_loop(0, total // BLOCK, project, 0)

    def query(i, carry):
        rows = pl.ds(pl.multiple_of(i * BLOCK, BLOCK), BLOCK)
        here = pl.ds(pl.multiple_of(i * BLOCK + W, BLOCK), BLOCK)
        q = contract(nx_ref[here, :], wq_ref[...], 1, 0)
        q = (q * cos_ref[here, :] + swap(q) * sin_ref[here, :]).astype(jnp.bfloat16)
        qs[rows, :] = q * jnp.bfloat16(SCORE_SCALE)
        return carry

    lax.fori_loop(0, own // BLOCK, query, 0)

    def visit(b, carry):
        rows = pl.ds(pl.multiple_of(b * BLOCK, BLOCK), BLOCK)
        here = pl.ds(pl.multiple_of(b * BLOCK + W, BLOCK), BLOCK)
        window = pl.ds(pl.multiple_of(b * BLOCK, BLOCK), SPAN)
        contexts, grads = [], []
        for h in range(2):
            mine = (lane // HD) == h
            kb = ks[window, :]
            vb = vs[window, :]
            qh = jnp.where(mine, qs[rows, :], jnp.bfloat16(0))
            gh = jnp.where(mine, do_ref[rows, :], jnp.bfloat16(0))
            s = contract(qh, kb, 1, 1) + bias[b]
            e = jnp.exp(s - jnp.max(s, axis=1, keepdims=True))
            w = e * (1.0 / jnp.sum(e, axis=1, keepdims=True))
            pb = w.astype(jnp.bfloat16)
            context = contract(pb, vb, 1, 0).astype(jnp.bfloat16)
            delta = jnp.sum(
                gh.astype(jnp.float32) * context.astype(jnp.float32), axis=1, keepdims=True
            )
            dp = contract(gh, vb, 1, 1)
            ds = (w * (dp - delta)).astype(jnp.bfloat16)
            contexts.append(context)
            grads.append(contract(ds, kb, 1, 0))
            dka[window, :] += contract(ds, qh, 0, 0)
            dva[window, :] += contract(pb, gh, 0, 0)
        first = lane < HD
        ctx_ref[rows, :] = jnp.where(first, contexts[0], contexts[1])
        g = jnp.where(first, grads[0], grads[1]) * SCORE_SCALE
        dq_ref[rows, :] = (g * cos_ref[here, :] - swap(g) * sin_ref[here, :]).astype(jnp.bfloat16)
        return carry

    lax.fori_loop(0, own // BLOCK, visit, 0)


def attention_kernel(
    core_ref, nx_ref, wq_ref, wk_ref, wv_ref, cos_ref, sin_ref, segq_ref, segk_ref, do_ref,
    ctx_ref, dq_ref, dk_ref, dv_ref,
    bias, qs, ks, vs, dka, dva,
):
    total = nx_ref.shape[0]
    lane = lax.broadcasted_iota(jnp.int32, (1, PAIR), 1)

    def swap(u):
        return swap_halves(u, lane)

    pair_attention(
        pl.program_id(0), nx_ref, wq_ref, wk_ref, wv_ref, cos_ref, sin_ref, segq_ref, segk_ref,
        do_ref, ctx_ref, dq_ref, bias, qs, ks, vs, dka, dva,
    )

    def finish(i, carry):
        rows = pl.ds(pl.multiple_of(i * BLOCK, BLOCK), BLOCK)
        g = dka[rows, :]
        dk_ref[rows, :] = (g * cos_ref[rows, :] - swap(g) * sin_ref[rows, :]).astype(jnp.bfloat16)
        dv_ref[rows, :] = dva[rows, :].astype(jnp.bfloat16)
        return carry

    lax.fori_loop(0, total // BLOCK, finish, 0)


def attention(core, nx, weights, cosine, sine, seg_q, seg_k, out_grads):
    total = nx.shape[0]
    own = total - W
    pairs = HALF // PAIR

    def whole(shape):
        return pl.BlockSpec(shape, lambda p, c: (0, 0))

    def columns(start):
        return pl.BlockSpec((D, PAIR), lambda p, c: (0, start + c[0] * pairs + p))

    def heads(rows):
        return pl.BlockSpec((rows, PAIR), lambda p, c: (0, p))

    return pl.pallas_call(
        attention_kernel,
        out_shape=[
            jax.ShapeDtypeStruct((own, HALF), jnp.bfloat16),
            jax.ShapeDtypeStruct((own, HALF), jnp.bfloat16),
            jax.ShapeDtypeStruct((total, HALF), jnp.bfloat16),
            jax.ShapeDtypeStruct((total, HALF), jnp.bfloat16),
        ],
        grid_spec=pltpu.PrefetchScalarGridSpec(
            num_scalar_prefetch=1,
            grid=(pairs,),
            in_specs=[
                whole((total, D)),
                columns(0),
                columns(2 * pairs),
                columns(4 * pairs),
                whole((total, PAIR)),
                whole((total, PAIR)),
                whole((own, 1)),
                whole((1, total)),
                heads(own),
            ],
            out_specs=[heads(own), heads(own), heads(total), heads(total)],
            scratch_shapes=[
                pltpu.VMEM((own // BLOCK, BLOCK, SPAN), jnp.float32),
                pltpu.VMEM((own, PAIR), jnp.bfloat16),
                pltpu.VMEM((total, PAIR), jnp.bfloat16),
                pltpu.VMEM((total, PAIR), jnp.bfloat16),
                pltpu.VMEM((total, PAIR), jnp.float32),
                pltpu.VMEM((total, PAIR), jnp.float32),
            ],
        ),
        compiler_params=pltpu.CompilerParams(vmem_limit_bytes=48 * 1024 * 1024),
        name="window_attention",
    )(core, nx, weights, weights, weights, cosine, sine, seg_q, seg_k, out_grads)


ROWS = 512
HALVES = 2
TABLE = HD // 2


def turn(angle):
    count = jnp.floor(angle * (2.0 / math.pi) + 0.5)
    r = angle - count * 1.5703125
    r = r - count * 4.837512969970703125e-4
    r = r - count * 7.54978995489188e-8
    z = r * r
    s = r + r * z * (-1.6666654611e-1 + z * (8.3321608736e-3 - z * 1.9515295891e-4))
    c = 1.0 - 0.5 * z + z * z * (4.166664568298827e-2 + z * (-1.388731625493765e-3 + z * 2.443315711809948e-5))
    quarter = count - 4.0 * jnp.floor(count * 0.25)
    odd = (quarter == 1.0) | (quarter == 3.0)
    sine = jnp.where(odd, c, s)
    cosine = jnp.where(odd, s, c)
    sine = jnp.where(quarter >= 2.0, -sine, sine)
    cosine = jnp.where((quarter == 1.0) | (quarter == 2.0), -cosine, cosine)
    return cosine, sine


def rotated(u, c, s):
    parts = []
    for h in range(2):
        a = u[h * HD : h * HD + TABLE]
        b = u[h * HD + TABLE : (h + 1) * HD]
        parts += [a * c - b * s, b * c + a * s]
    return jnp.concatenate(parts, axis=0)


class Unit:
    pass


def attend(blocks, bias, qT, kT, vT, ks, vs, gT, ctxT, dqT, dkT, dvT):
    chunks = SPAN // BLOCK
    sub = lax.broadcasted_iota(jnp.int32, (PAIR, 1), 0)
    bf16, f32 = jnp.bfloat16, jnp.float32

    def unit(b, h):
        u = Unit()
        u.b, u.h = b, h
        u.cols = pl.ds(pl.multiple_of(b * BLOCK, BLOCK), BLOCK)
        u.head = slice(h * HD, (h + 1) * HD)
        u.mine = (sub // HD) == h
        return u

    def keys(u, c):
        return pl.ds(pl.multiple_of(u.b * BLOCK + c * BLOCK, BLOCK), BLOCK)

    def score(u, c):
        if c == 0:
            q = qT[:, u.cols]
            u.q, u.qh, u.s = jnp.where(u.mine, q, bf16(0)), q[u.head], []
        s = contract(ks[keys(u, c), :], u.q, 1, 0) + bias[u.b, c * BLOCK : (c + 1) * BLOCK, :]
        u.s.append(s)
        top = jnp.max(s.reshape(-1, 8, BLOCK), axis=0)
        u.m = top if c == 0 else jnp.maximum(u.m, top)
        if c == chunks - 1:
            u.m = jnp.max(u.m, axis=0, keepdims=True)

    def expand(u, c):
        if c == 0:
            u.e = []
        e = jnp.exp(u.s[c] - u.m)
        u.e.append(e)
        part = jnp.sum(e.reshape(-1, 8, BLOCK), axis=0)
        u.l = part if c == 0 else u.l + part
        if c == chunks - 1:
            u.inv = 1.0 / jnp.sum(u.l, axis=0, keepdims=True)

    def mix(u, c):
        if c == 0:
            u.w, u.p = [], []
        w = u.e[c] * u.inv
        u.w.append(w)
        u.p.append(w.astype(bf16))
        t = contract(vT[u.head, keys(u, c)], u.p[c], 1, 0)
        u.ctx = t if c == 0 else u.ctx + t
        if c == chunks - 1:
            g = gT(u.cols)
            u.g, u.gh = jnp.where(u.mine, g, bf16(0)), g[u.head]
            u.ctx = u.ctx.astype(bf16)
            ctxT[u.head, u.cols] = u.ctx
            u.delta = jnp.sum(u.gh.astype(f32) * u.ctx.astype(f32), axis=0, keepdims=True)

    def slope(u, c):
        if c == 0:
            u.ds = []
        dp = contract(vs[keys(u, c), :], u.g, 1, 0)
        u.ds.append((u.w[c] * (dp - u.delta)).astype(bf16))
        dvT[u.head, keys(u, c)] += contract(u.gh, u.p[c], 1, 1)

    def back(u, c):
        t = contract(kT[u.head, keys(u, c)], u.ds[c], 1, 0)
        u.dq = t if c == 0 else u.dq + t
        dkT[u.head, keys(u, c)] += contract(u.qh, u.ds[c], 1, 1)
        if c == chunks - 1:
            dqT[u.head, u.cols] = u.dq

    stages = [score, expand, mix, slope, back]
    units = [unit(b, h) for b in blocks for h in range(2)]
    for t in range(len(stages) + len(units) - 1):
        for c in range(chunks):
            for n, u in enumerate(units):
                if 0 <= t - n < len(stages):
                    stages[t - n](u, c)


def whole_kernel(
    x_ref, w_ref, pos_ref, seg_ref, g_ref, freq_ref,
    ctx_ref, ig_ref, pg_ref,
    nx, rms, wg, wpack, wT, meta, metag, gsend, gbuf, gT, cosT, sinT, segc, bias,
    qT, kT, vT, ks, vs, ctxT, dqT, dkT, dvT, dqb, dkvb, dtok,
    ctxs, ctxr, part, sums, decks, kept, give, got, ps, pr, fwd, later, ys, yr, ngo,
    w_send, w_recv, x_send, x_recv, m_send, m_recv, g_send, g_recv,
    part_send, part_recv, deck_send, deck_recv, ctx_send, ctx_recv, n_send, n_recv,
    *, count, grad_scale,
):
    f32, bf16 = jnp.float32, jnp.bfloat16
    me = lax.axis_index("seq")
    core = lax.rem(me, 2)
    chip = lax.div(me, 2)
    chips = count // 2
    layers = count // 4
    partner = me + 1 - 2 * core
    side = lax.rem(chip, 2)
    layer = lax.div(chip, 2)
    share = D // count
    group = lax.axis_index("groups")
    mine_at = pl.multiple_of(core * ROWS, ROWS)
    other_at = pl.multiple_of((1 - core) * ROWS, ROWS)
    has_prev = chip > 0
    has_next = chip < chips - 1
    prev = lax.rem(me + count - 2, count)
    after = lax.rem(me + 2, count)

    def remote(source, target, send, recv, device, part_of=None):
        return pltpu.make_async_remote_copy(
            src_ref=source, dst_ref=target, send_sem=send, recv_sem=recv,
            device_id={"groups": group if part_of is None else part_of, "seq": device},
            device_id_type=pl.DeviceIdType.MESH,
        )

    def place(z, x, c):
        return (z * 2 + x) * 2 + c

    barrier = pltpu.get_barrier_semaphore()

    def greet(i, carry):
        pl.semaphore_signal(
            barrier, inc=1, device_id={"groups": group, "seq": lax.rem(me + 1 + i, count)},
            device_id_type=pl.DeviceIdType.MESH,
        )
        return carry

    lax.fori_loop(0, count - 1, greet, 0)
    pl.semaphore_signal(
        barrier, inc=1, device_id={"groups": 1 - group, "seq": me}, device_id_type=pl.DeviceIdType.MESH
    )

    for p in range(3):
        for h in range(2):
            wpack[p, h] = jnp.concatenate(
                [w_ref[:, t * D + h * HALF + p * PAIR : t * D + h * HALF + (p + 1) * PAIR] for t in range(3)],
                axis=1,
            )

    meta[0:1, :] = pos_ref[...]
    meta[1:2, :] = seg_ref[...]
    metag[2 + core] = meta[...]

    own_block = pl.ds(pl.multiple_of(me * share, share), share)
    for p in range(3):
        wg[p, own_block, :] = wpack[p, core]

    def block_of(device):
        return pl.ds(pl.multiple_of(device * share, share), share)

    planes = 2 * layers - 1

    def w_near(p, j):
        hop, shift = lax.div(j + 1, 2), lax.rem(j + 1, 2)
        to = lax.rem(core + shift, 2)
        return remote(
            wpack.at[p, to], wg.at[p, own_block, :], w_send.at[p, j], w_recv.at[p, 2 * layer + core],
            place(lax.rem(layer + hop, layers), side, to),
        )

    def w_near_arrival(p, j):
        hop, shift = lax.div(j + 1, 2), lax.rem(j + 1, 2)
        z, c = lax.rem(layer + layers - hop, layers), lax.rem(core + shift, 2)
        device = place(z, side, c)
        return remote(
            wpack.at[p, 0], wg.at[p, block_of(device), :], w_send.at[p, j], w_recv.at[p, 2 * z + c], device
        )

    def w_cross(p, c):
        return remote(
            wpack.at[p, c], wg.at[p, own_block, :], w_send.at[p, planes + c],
            w_recv.at[p, 2 * layers + layer], place(layer, 1 - side, c),
        )

    def crossed(z):
        return block_of(place(z, 1 - side, group))

    def w_around(p, hop):
        return remote(
            wg.at[p, crossed(layer), :], wg.at[p, crossed(layer), :], w_send.at[p, planes + 1 + hop],
            w_recv.at[p, 2 * layers + layer], place(lax.rem(layer + hop, layers), side, core),
        )

    def w_arrival(p, hop):
        z = lax.rem(layer + layers - hop, layers)
        return remote(
            wg.at[p, crossed(z), :], wg.at[p, crossed(z), :], w_send.at[p, planes + 2],
            w_recv.at[p, 2 * layers + z], partner,
        )

    def w_over(p, hop):
        z = lax.rem(layer + layers - hop, layers)
        return remote(
            wg.at[p, crossed(z), :], wg.at[p, crossed(z), :], w_send.at[p, planes + layers + 1 + hop],
            w_recv.at[p, 3 * layers + z], me, 1 - group,
        )

    def w_over_arrival(p, z):
        rows = block_of(place(z, 1 - side, 1 - group))
        return remote(
            wg.at[p, rows, :], wg.at[p, rows, :], w_send.at[p, planes + 2], w_recv.at[p, 3 * layers + z],
            me, 1 - group,
        )

    def loop(n, body):
        def step(i, carry):
            body(i)
            return carry

        lax.fori_loop(0, n, step, 0)

    def send_weights(p):
        @pl.when(core == group)
        def _():
            for c in range(2):
                w_cross(p, c).start()

        loop(planes, lambda j: w_near(p, j).start())

    def relay_first(p):
        w_arrival(p, 0).wait_recv()
        loop(layers - 1, lambda j: w_around(p, j + 1).start())
        w_over(p, 0).start()

    def relay_rest(p):
        def step(j):
            w_arrival(p, j + 1).wait_recv()
            w_over(p, j + 1).start()

        loop(layers - 1, step)

    def await_weights(p):
        loop(planes, lambda j: w_near_arrival(p, j).wait_recv())
        loop(layers, lambda z: w_over_arrival(p, z).wait_recv())

    mine_rows = pl.ds(pl.multiple_of(W + mine_at, ROWS), ROWS)
    other_rows = pl.ds(pl.multiple_of(W + other_at, ROWS), ROWS)

    def chunk_rows(base, k):
        return pl.ds(pl.multiple_of(base + k * BLOCK, BLOCK), BLOCK)

    def x_swap():
        return remote(nx.at[mine_rows], nx.at[mine_rows], x_send.at[0], x_recv.at[0], partner)

    def x_swap_arrival():
        return remote(nx.at[other_rows], nx.at[other_rows], x_send.at[0], x_recv.at[0], partner)

    def x_next(k):
        return remote(
            nx.at[chunk_rows(W + mine_at, k)], nx.at[chunk_rows(mine_at, k)],
            x_send.at[1 + k], x_recv.at[1 + k], after,
        )

    def x_relay(k):
        return remote(
            nx.at[chunk_rows(mine_at, k)], nx.at[chunk_rows(mine_at, k)],
            x_send.at[3 + k], x_recv.at[3 + k], partner,
        )

    def x_relay_arrival(k):
        return remote(
            nx.at[chunk_rows(other_at, k)], nx.at[chunk_rows(other_at, k)],
            x_send.at[3 + k], x_recv.at[3 + k], partner,
        )

    def m_swap():
        return remote(metag.at[2 + core], metag.at[2 + core], m_send.at[0], m_recv.at[0], partner)

    def m_swap_arrival():
        return remote(metag.at[3 - core], metag.at[3 - core], m_send.at[0], m_recv.at[0], partner)

    def m_next(t):
        device = after - core + t
        return remote(meta, metag.at[core], m_send.at[1 + t], m_recv.at[1 + core], device)

    def m_prev_arrival(t):
        return remote(meta, metag.at[t], m_send.at[1 + t], m_recv.at[1 + t], prev)

    def g_swap():
        return remote(gsend, gbuf.at[pl.ds(mine_at, ROWS), :], g_send, g_recv, partner)

    def g_arrival():
        return remote(gsend, gbuf.at[pl.ds(other_at, ROWS), :], g_send, g_recv, partner)

    half_mine = pl.ds(pl.multiple_of(core * HALF, HALF), HALF)
    half_other = pl.ds(pl.multiple_of((1 - core) * HALF, HALF), HALF)
    gsend[...] = g_ref[:, half_other]
    gbuf[pl.ds(mine_at, ROWS), :] = g_ref[:, half_mine]

    def normalize(k):
        rows = pl.ds(pl.multiple_of(k * BLOCK, BLOCK), BLOCK)
        x = x_ref[rows, :].astype(f32)
        inv = lax.rsqrt(jnp.mean(x * x, axis=1, keepdims=True) + EPSILON)
        rms[rows, :] = inv
        nx[chunk_rows(W + mine_at, k), :] = (x * inv).astype(bf16)

    loop(2, normalize)

    pl.semaphore_wait(barrier, count)
    send_weights(0)
    m_swap().start()
    x_swap().start()
    g_swap().start()

    def forward_tokens(c):
        @pl.when(has_next & (core == c))
        def _():
            x_next(1).start()
            x_next(0).start()

    @pl.when(has_next)
    def _():
        m_next(0).start()
        m_next(1).start()

    forward_tokens(1)
    relay_first(0)
    relay_rest(0)
    forward_tokens(0)
    send_weights(1)
    send_weights(2)

    @pl.when(has_prev)
    def _():
        m_prev_arrival(0).wait_recv()
        m_prev_arrival(1).wait_recv()

    @pl.when(jnp.logical_not(has_prev))
    def _():
        row = lax.broadcasted_iota(jnp.int32, (8, ROWS), 0)
        gone = jnp.where(row == 1, -1, 0)
        metag[0] = gone
        metag[1] = gone
        nx[:W, :] = jnp.zeros((W, D), bf16)

    m_swap_arrival().wait_recv()
    g_arrival().wait_recv()

    for n in range(4):
        angle = metag[n][0:1, :].astype(f32) * freq_ref[:, 0:1]
        c, s = turn(angle)
        cosT[:, n * ROWS : (n + 1) * ROWS] = c
        sinT[:, n * ROWS : (n + 1) * ROWS] = s
        seg = metag[n][1:2, :].astype(f32)
        for j in range(ROWS // PAIR):
            flat = jnp.broadcast_to(seg[:, j * PAIR : (j + 1) * PAIR], (PAIR, PAIR))
            segc[n * ROWS + j * PAIR : n * ROWS + (j + 1) * PAIR, :] = jnp.transpose(flat)
    for n in range(2):
        gT[:, n * ROWS : (n + 1) * ROWS] = jnp.transpose(gbuf[n * ROWS : (n + 1) * ROWS, :])

    key = lax.broadcasted_iota(jnp.int32, (BLOCK, BLOCK), 0)
    query = lax.broadcasted_iota(jnp.int32, (BLOCK, BLOCK), 1)
    for b in range(W // BLOCK):
        at = b * BLOCK
        seg_q = metag[2 + at // ROWS][1:2, at % ROWS : at % ROWS + BLOCK].astype(f32)
        for c in range(SPAN // BLOCK):
            seg_k = segc[at + c * BLOCK : at + (c + 1) * BLOCK, :]
            same = jnp.concatenate([seg_k == seg_q[:, :PAIR], seg_k == seg_q[:, PAIR:]], axis=1)
            if c == 0:
                same = same & (key > query)
            if c == SPAN // BLOCK - 1:
                same = same & (key <= query)
            bias[b, c * BLOCK : (c + 1) * BLOCK, :] = jnp.where(same, 0.0, MASKED_SCORE)

    relay_first(1)
    relay_first(2)

    def table(n):
        cols = pl.ds(pl.multiple_of(n * BLOCK, BLOCK), BLOCK)
        return cols, cosT[:, cols], sinT[:, cols]

    def project_before(n):
        cols, c, s = table(n)
        kv = contract(wT[PAIR:, :], nx[cols, :], 1, 1)
        k = rotated(kv[:PAIR], c, s).astype(bf16)
        v = kv[PAIR:].astype(bf16)
        kT[:, cols] = k
        vT[:, cols] = v
        ks[cols, :] = jnp.transpose(k)
        vs[cols, :] = jnp.transpose(v)

    def project_own(i):
        n = i + W // BLOCK
        cols, c, s = table(n)
        at = pl.ds(pl.multiple_of(i * BLOCK, BLOCK), BLOCK)
        qkv = contract(wT[...], nx[cols, :], 1, 1)
        qT[:, at] = rotated(qkv[:PAIR], c, s).astype(bf16) * bf16(SCORE_SCALE)
        k = rotated(qkv[PAIR : 2 * PAIR], c, s).astype(bf16)
        v = qkv[2 * PAIR :].astype(bf16)
        kT[:, cols] = k
        vT[:, cols] = v
        ks[cols, :] = jnp.transpose(k)
        vs[cols, :] = jnp.transpose(v)

    def finish_chunk(p, n):
        cols, c, s = table(n)
        k = rotated(dkT[:, cols], c, -s).astype(bf16)
        v = dvT[:, cols].astype(bf16)
        kv = jnp.concatenate([k, v], axis=0)
        dkvb[:, cols] = kv
        dtok[p, cols, PAIR:] = jnp.transpose(kv)

    def finish_query(p, i):
        cols, c, s = table(i + W // BLOCK)
        at = pl.ds(pl.multiple_of(i * BLOCK, BLOCK), BLOCK)
        q = rotated(dqT[:, at] * SCORE_SCALE, c, -s).astype(bf16)
        dqb[:, at] = q
        dtok[p, cols, :PAIR] = jnp.transpose(q)
        ctxs[p, at, :] = jnp.transpose(ctxT[:, at])

    def ctx_copy(p):
        return remote(
            ctxs.at[p, pl.ds(other_at, ROWS), :], ctxr.at[p], ctx_send.at[p], ctx_recv.at[p], partner
        )

    deck = 4 * share

    def layer_rows(z):
        return pl.ds(pl.multiple_of(z * deck, deck), deck)

    def part_copy(p, hop):
        z = lax.rem(layer + hop, layers)
        return remote(
            part.at[p, layer_rows(z), :], sums.at[p, hop - 1],
            part_send.at[p, hop - 1], part_recv.at[p, hop - 1], place(z, side, core),
        )

    def peer(k):
        return [(side, 1 - core), (1 - side, core), (1 - side, 1 - core)][k]

    def deck_copy(p, k):
        x, c = peer(k)
        return remote(
            give.at[p, k], got.at[p, k], deck_send.at[p, k], deck_recv.at[p, k], place(layer, x, c)
        )

    def share_out(p):
        for hop in range(1, layers):
            part_copy(p, hop).wait_recv()
        total = part[p, layer_rows(layer), :].astype(f32)
        for hop in range(1, layers):
            total = total + sums[p, hop - 1].astype(f32)
        decks[...] = total

        def rows(x, c):
            return decks[pl.ds(pl.multiple_of((2 * x + c) * share, share), share), :]

        kept[p] = rows(side, core)
        for k in (1, 2, 0):
            give[p, k] = rows(*peer(k)).astype(bf16)
            deck_copy(p, k).start()

    def collect(p):
        for k in range(3):
            deck_copy(p, k).wait_recv()
        even = kept[p] + got[p, 1].astype(f32)
        odd = got[p, 0].astype(f32) + got[p, 2].astype(f32)
        for t in range(3):
            at = t * D + p * PAIR
            a = pl.ds(pl.multiple_of(at + core * HALF, PAIR), PAIR)
            b = pl.ds(pl.multiple_of(at + (1 - core) * HALF, PAIR), PAIR)
            pg_ref[:, a] = even[:, t * PAIR : (t + 1) * PAIR] * grad_scale
            pg_ref[:, b] = odd[:, t * PAIR : (t + 1) * PAIR] * grad_scale

    def n_swap(k):
        return remote(ps.at[k], pr.at[k], n_send.at[k], n_recv.at[k], partner)

    def n_back(k):
        return remote(fwd.at[k], later.at[k], n_send.at[2 + k], n_recv.at[2 + k], prev)

    def n_own():
        return remote(ys, yr, n_send.at[4], n_recv.at[4], partner)

    def before_grad(half, k):
        rows = chunk_rows(half * ROWS, k)
        return sum(
            contract(dtok[p, rows, PAIR:], wg[p, :, PAIR:], 1, 1) for p in range(3)
        )

    def give_before(half):
        owner = core == half

        def step(k):
            mine = before_grad(half, k)

            @pl.when(jnp.logical_not(owner))
            def _():
                ps[k] = mine.astype(bf16)
                n_swap(k).start()

            @pl.when(owner)
            def _():
                ngo[pl.ds(pl.multiple_of(k * BLOCK, BLOCK), BLOCK), :] = mine

        loop(2, step)

    def pass_before(half):
        @pl.when(core == half)
        def _():
            for k in range(2):
                n_swap(k).wait_recv()
                fwd[k] = (ngo[k * BLOCK : (k + 1) * BLOCK, :] + pr[k].astype(f32)).astype(bf16)

                @pl.when(has_prev)
                def _():
                    n_back(k).start()

    def own_grad(at, k):
        rows = chunk_rows(W + at, k)
        return sum(contract(dtok[p, rows, :], wg[p], 1, 1) for p in range(3))

    def step(t):
        p = lax.div(t, 2)
        i = lax.rem(t, 2)
        half = jnp.where(p == 0, 1 - i, i)

        @pl.when(i == 0)
        def _():
            await_weights(p)
            wT[...] = jnp.transpose(wg[p])

            @pl.when(p == 0)
            def _():
                x_swap_arrival().wait_recv()

            loop(4, project_own)

            @pl.when(p > 0)
            def _():
                loop(4, project_before)

            dkT[...] = jnp.zeros_like(dkT)
            dvT[...] = jnp.zeros_like(dvT)

        @pl.when(p == 0)
        def _():
            @pl.when(has_prev)
            def _():
                @pl.when(core == half)
                def _():
                    for k in (1, 0):
                        x_next(k).wait_recv()
                        x_relay(k).start()

                @pl.when(core != half)
                def _():
                    for k in (1, 0):
                        x_relay_arrival(k).wait_recv()

            loop(2, lambda k: project_before(half * 2 + k))

        attend(
            [half * 2, half * 2 + 1], bias, qT, kT, vT, ks, vs,
            lambda cols: gT[pl.ds(pl.multiple_of(p * PAIR, PAIR), PAIR), cols],
            ctxT, dqT, dkT, dvT,
        )

        @pl.when(t < 2)
        def _():
            relay_rest(t + 1)

        @pl.when((t == 2) | (t == 4))
        def _():
            share_out(p - 1)

        @pl.when(t == 4)
        def _():
            loop(2, lambda n: finish_chunk(p, n))
            give_before(0)

        @pl.when(i == 1)
        def _():
            @pl.when(p == 2)
            def _():
                pass_before(0)
                loop(2, lambda n: finish_chunk(p, n + 2))
                give_before(1)

            @pl.when(p < 2)
            def _():
                loop(4, lambda n: finish_chunk(p, n))

            loop(4, lambda n: finish_chunk(p, n + 4))
            loop(4, lambda n: finish_query(p, n))

            kv = contract(dkvb[...], nx[...], 1, 0)
            q = contract(dqb[...], nx[W:, :], 1, 0)
            part[p, :, :PAIR] = jnp.transpose(q.astype(bf16))
            part[p, :, PAIR:] = jnp.transpose(kv.astype(bf16))

            @pl.when(p == 2)
            def _():
                pass_before(1)

            for hop in (2, 1, 3):
                part_copy(p, hop).start()
            ctx_copy(p).start()

    loop(6, step)

    def give_own(k):
        ys[pl.ds(pl.multiple_of(k * BLOCK, BLOCK), BLOCK), :] = own_grad(other_at, k).astype(bf16)

    loop(2, give_own)
    n_own().start()

    def keep_own(k):
        ngo[pl.ds(pl.multiple_of(k * BLOCK, BLOCK), BLOCK), :] = own_grad(mine_at, k)

    loop(2, keep_own)

    for p in range(3):
        ctx_copy(p).wait()
        mine_cols = pl.ds(pl.multiple_of(core * HALF + p * PAIR, PAIR), PAIR)
        other_cols = pl.ds(pl.multiple_of((1 - core) * HALF + p * PAIR, PAIR), PAIR)
        ctx_ref[:, mine_cols] = ctxs[p, pl.ds(mine_at, ROWS), :]
        ctx_ref[:, other_cols] = ctxr[p]

    collect(0)
    collect(1)
    share_out(2)
    n_own().wait()

    @pl.when(has_next)
    def _():
        n_back(0).wait_recv()
        n_back(1).wait_recv()

    @pl.when(jnp.logical_not(has_next))
    def _():
        later[...] = jnp.zeros_like(later)

    def finish(k):
        rows = pl.ds(pl.multiple_of(k * BLOCK, BLOCK), BLOCK)
        ng = ngo[rows, :] + yr[rows, :].astype(f32) + later[k].astype(f32)
        inv = rms[rows, :]
        scaled = x_ref[rows, :].astype(f32) * inv
        ig_ref[rows, :] = (
            inv * (ng - scaled * jnp.mean(ng * scaled, axis=1, keepdims=True))
        ).astype(bf16)

    loop(2, finish)
    collect(2)

    for p in range(3):
        @pl.when(core == group)
        def _():
            for c in range(2):
                w_cross(p, c).wait_send()

        loop(planes, lambda j: w_near(p, j).wait_send())
        loop(layers - 1, lambda j: w_around(p, j + 1).wait_send())
        loop(layers, lambda j: w_over(p, j).wait_send())
        for hop in range(1, layers):
            part_copy(p, hop).wait_send()
        for k in range(3):
            deck_copy(p, k).wait_send()
    m_swap().wait_send()
    x_swap().wait_send()
    g_swap().wait_send()

    @pl.when(has_next)
    def _():
        for k in range(2):
            m_next(k).wait_send()
            x_next(k).wait_send()

    @pl.when(has_prev)
    def _():
        for k in range(2):
            x_relay(k).wait_send()
            n_back(k).wait_send()

    for k in range(2):
        n_swap(k).wait_send()


def whole(count, grad_scale, x, weights, positions, segments, out_grads):
    share = D // count
    bf16, f32 = jnp.bfloat16, jnp.float32
    total = 2 * W
    vmem = pl.BlockSpec(memory_space=pltpu.VMEM)
    frequency = np.exp(np.float32(-math.log(10000.0)) * np.arange(TABLE, dtype=np.float32) / np.float32(TABLE))
    frequency = np.broadcast_to(frequency.astype(np.float32)[:, None], (TABLE, PAIR))
    dma = pltpu.SemaphoreType.DMA
    layers = count // 4
    planes = 2 * layers - 1
    return pl.pallas_call(
        functools.partial(whole_kernel, count=count, grad_scale=grad_scale),
        out_shape=[
            jax.ShapeDtypeStruct((ROWS, D), bf16),
            jax.ShapeDtypeStruct((ROWS, D), bf16),
            jax.ShapeDtypeStruct((share, 3 * D), f32),
        ],
        in_specs=[vmem] * 6,
        out_specs=[vmem] * 3,
        scratch_shapes=[
            pltpu.VMEM((total, D), bf16),
            pltpu.VMEM((ROWS, 1), f32),
            pltpu.VMEM((3, D, 3 * PAIR), bf16),
            pltpu.VMEM((3, 2, share, 3 * PAIR), bf16),
            pltpu.VMEM((3 * PAIR, D), bf16),
            pltpu.VMEM((8, ROWS), jnp.int32),
            pltpu.VMEM((4, 8, ROWS), jnp.int32),
            pltpu.VMEM((ROWS, HALF), bf16),
            pltpu.VMEM((W, HALF), bf16),
            pltpu.VMEM((HALF, W), bf16),
            pltpu.VMEM((TABLE, total), f32),
            pltpu.VMEM((TABLE, total), f32),
            pltpu.VMEM((total, PAIR), f32),
            pltpu.VMEM((W // BLOCK, SPAN, BLOCK), f32),
            pltpu.VMEM((PAIR, W), bf16),
            pltpu.VMEM((PAIR, total), bf16),
            pltpu.VMEM((PAIR, total), bf16),
            pltpu.VMEM((total, PAIR), bf16),
            pltpu.VMEM((total, PAIR), bf16),
            pltpu.VMEM((PAIR, W), bf16),
            pltpu.VMEM((PAIR, W), f32),
            pltpu.VMEM((PAIR, total), f32),
            pltpu.VMEM((PAIR, total), f32),
            pltpu.VMEM((PAIR, W), bf16),
            pltpu.VMEM((2 * PAIR, total), bf16),
            pltpu.VMEM((3, total, 3 * PAIR), bf16),
            pltpu.VMEM((3, W, PAIR), bf16),
            pltpu.VMEM((3, ROWS, PAIR), bf16),
            pltpu.VMEM((3, D, 3 * PAIR), bf16),
            pltpu.VMEM((3, layers - 1, 4 * share, 3 * PAIR), bf16),
            pltpu.VMEM((4 * share, 3 * PAIR), f32),
            pltpu.VMEM((3, share, 3 * PAIR), f32),
            pltpu.VMEM((3, 3, share, 3 * PAIR), bf16),
            pltpu.VMEM((3, 3, share, 3 * PAIR), bf16),
            pltpu.VMEM((2, BLOCK, D), bf16),
            pltpu.VMEM((2, BLOCK, D), bf16),
            pltpu.VMEM((2, BLOCK, D), bf16),
            pltpu.VMEM((2, BLOCK, D), bf16),
            pltpu.VMEM((ROWS, D), bf16),
            pltpu.VMEM((ROWS, D), bf16),
            pltpu.VMEM((ROWS, D), f32),
            dma((3, planes + 2 * layers + 1)), dma((3, 4 * layers)),
            dma((5,)), dma((5,)),
            dma((3,)), dma((3,)),
            dma, dma,
            dma((3, layers - 1)), dma((3, layers - 1)),
            dma((3, 3)), dma((3, 3)),
            dma((3,)), dma((3,)),
            dma((5,)), dma((5,)),
        ],
        compiler_params=pltpu.CompilerParams(
            vmem_limit_bytes=60 * 1024 * 1024, collective_id=0, has_side_effects=True
        ),
        name="whole_sublayer",
    )(x, weights, positions, segments, out_grads, frequency)


def swapped(value):
    count = lax.axis_size("seq")
    return lax.ppermute(value, "seq", [(s, s ^ 1) for s in range(count)])


def chip_shifted(value, steps):
    count = lax.axis_size("seq")
    pairs = [(s, s + 2 * steps) for s in range(count) if 0 <= s + 2 * steps < count]
    return lax.ppermute(value, "seq", pairs)


def ordered(core, mine, other, axis=0):
    first = jnp.where(core == 0, mine, other)
    second = jnp.where(core == 0, other, mine)
    return jnp.concatenate([first, second], axis=axis)


def local(inputs, projection, positions, segments, context_grad):
    row_count = inputs.shape[0]
    device_count = lax.axis_size("seq")
    chips = device_count // 2
    device_index = lax.axis_index("seq")
    core = device_index % 2
    chip = device_index // 2
    assert 2 * row_count == W
    grad_scale = (row_count * device_count) ** (-0.5)

    if (D // device_count) % 16 == 0:
        return tuple(
            whole(
                device_count, grad_scale, inputs, projection, positions[None, :], segments[None, :],
                context_grad,
            )
        )

    weights = lax.all_gather(projection, "seq", axis=0, tiled=True)

    meta = jnp.stack([positions, segments], axis=0)
    x_before = chip_shifted(inputs, 1)
    meta_before = chip_shifted(meta, 1)
    x_other = swapped(inputs)
    meta_other = swapped(meta)
    x_before_other = swapped(x_before)
    meta_before_other = swapped(meta_before)
    grad_mine = lax.dynamic_slice_in_dim(context_grad, core * HALF, HALF, 1)
    grad_sent = lax.dynamic_slice_in_dim(context_grad, (1 - core) * HALF, HALF, 1)
    grad_other = swapped(grad_sent)
    out_grads = ordered(core, grad_mine, grad_other)

    x_all = jnp.concatenate(
        [ordered(core, x_before, x_before_other), ordered(core, inputs, x_other)], axis=0
    ).astype(jnp.float32)
    nx = (
        x_all * lax.rsqrt(jnp.mean(x_all * x_all, axis=1, keepdims=True) + EPSILON)
    ).astype(jnp.bfloat16)
    meta_all = jnp.concatenate(
        [ordered(core, meta_before, meta_before_other, 1), ordered(core, meta, meta_other, 1)],
        axis=1,
    )
    half_size = HD // 2
    frequency = jnp.exp(-math.log(10000.0) * jnp.arange(half_size, dtype=jnp.float32) / half_size)
    angle = meta_all[0].astype(jnp.float32)[:, None] * frequency[None, :]
    c, s = jnp.cos(angle), jnp.sin(angle)
    cosine = jnp.concatenate([c, c, c, c], axis=1)
    sine = jnp.concatenate([-s, s, -s, s], axis=1)
    seg_all = meta_all[1]
    outside = (jnp.arange(seg_all.shape[0]) < W) & (chip == 0)
    seg_k = jnp.where(outside, -1, seg_all)[None, :]
    seg_q = seg_all[W:][:, None]

    x_float = inputs.astype(jnp.float32)
    inv_rms = lax.rsqrt(jnp.mean(x_float * x_float, axis=1, keepdims=True) + EPSILON)
    scaled = x_float * inv_rms

    context_heads, dq, dk, dv = attention(
        core.astype(jnp.int32)[None], nx, weights, cosine, sine, seg_q, seg_k, out_grads
    )

    mine_at = core * row_count
    other_at = (1 - core) * row_count
    context_mine = lax.dynamic_slice_in_dim(context_heads, mine_at, row_count, 0)
    context_other = swapped(lax.dynamic_slice_in_dim(context_heads, other_at, row_count, 0))
    context = ordered(core, context_mine, context_other, 1)

    w_q, w_k, w_v = [
        lax.dynamic_slice_in_dim(weights, t * D + core * HALF, HALF, 1) for t in range(3)
    ]
    dkv = jnp.concatenate([dk, dv], axis=1)
    w_kv = jnp.concatenate([w_k, w_v], axis=1)
    ng_kv = contract(dkv, w_kv, 1, 1)
    ng_q = contract(dq, w_q, 1, 1)
    ng_before = ng_kv[:W]
    ng_own = ng_kv[W:] + ng_q
    send_before = lax.dynamic_slice_in_dim(ng_before, other_at, row_count, 0).astype(jnp.bfloat16)
    keep_before = lax.dynamic_slice_in_dim(ng_before, mine_at, row_count, 0)
    before = keep_before + swapped(send_before).astype(jnp.float32)
    later = chip_shifted(before.astype(jnp.bfloat16), -1)
    send_own = lax.dynamic_slice_in_dim(ng_own, other_at, row_count, 0).astype(jnp.bfloat16)
    keep_own = lax.dynamic_slice_in_dim(ng_own, mine_at, row_count, 0)
    normed_grad = (
        keep_own + swapped(send_own).astype(jnp.float32) + later.astype(jnp.float32)
    )
    input_grad = (
        inv_rms * (normed_grad - scaled * jnp.mean(normed_grad * scaled, axis=1, keepdims=True))
    ).astype(jnp.bfloat16)

    pg_kv = contract(nx, dkv, 0, 0)
    pg_q = contract(nx[W:], dq, 0, 0)
    pg = jnp.concatenate([pg_q, pg_kv], axis=1).astype(jnp.bfloat16)
    groups = [[2 * i + k for i in range(chips)] for k in range(2)]
    summed = lax.psum_scatter(
        pg, "seq", scatter_dimension=0, axis_index_groups=groups, tiled=True
    ).astype(jnp.float32)
    rows = summed.shape[0] // 2
    keep = lax.dynamic_slice_in_dim(summed, core * rows, rows, 0)
    other = swapped(lax.dynamic_slice_in_dim(summed, (1 - core) * rows, rows, 0).astype(jnp.bfloat16))
    other = other.astype(jnp.float32)
    parts = []
    for t in range(3):
        cols = slice(t * HALF, (t + 1) * HALF)
        parts.append(ordered(core, keep[:, cols], other[:, cols], 1))
    projection_grad = jnp.concatenate(parts, axis=1) * grad_scale
    return (context, input_grad, projection_grad)


def solution(mesh):
    in_specs = (
        P(("groups", "seq"), None),
        P("seq", None),
        P(("groups", "seq")),
        P(("groups", "seq")),
        P(("groups", "seq"), None),
    )
    out_specs = (P(("groups", "seq"), None), P(("groups", "seq"), None), P(("groups", "seq"), None))
    return jax.shard_map(local, mesh=mesh, in_specs=in_specs, out_specs=out_specs, check_vma=False)
```

```python
import functools
import math

import jax
import jax.numpy as jnp
import numpy as np
from jax import lax
from jax.experimental import pallas as pl
from jax.experimental.pallas import tpu as pltpu
from jax.sharding import PartitionSpec as P

D = 768
H = 12
HD = 64
W = 1024
EPSILON = 1e-05
SCORE_SCALE = 0.125
MASKED_SCORE = -1e30
BLOCK = 256
SPAN = BLOCK + W
PAIR = 2 * HD
HALF = D // 2


def contract(a, b, da, db):
    return lax.dot_general(a, b, (((da,), (db,)), ((), ())), preferred_element_type=jnp.float32)


def swap_halves(u, lane):
    low = (lane % HD) < HD // 2
    return jnp.where(low, pltpu.roll(u, PAIR - HD // 2, 1), pltpu.roll(u, HD // 2, 1))


def pair_attention(
    p, nx_ref, wq_ref, wk_ref, wv_ref, cos_ref, sin_ref, segq_ref, segk_ref, do_ref,
    ctx_ref, dq_ref,
    bias, qs, ks, vs, dka, dva,
):
    own = ctx_ref.shape[0]
    total = nx_ref.shape[0]
    lane = lax.broadcasted_iota(jnp.int32, (1, PAIR), 1)

    def swap(u):
        return swap_halves(u, lane)

    @pl.when(p == 0)
    def _():
        row = lax.broadcasted_iota(jnp.int32, (BLOCK, SPAN), 0)
        col = lax.broadcasted_iota(jnp.int32, (BLOCK, SPAN), 1)
        near = (col > row) & (col <= row + W)
        for b in range(own // BLOCK):
            same = segq_ref[b * BLOCK : (b + 1) * BLOCK, :] == segk_ref[:, b * BLOCK : b * BLOCK + SPAN]
            bias[b] = jnp.where(near & same, 0.0, MASKED_SCORE)

    def project(i, carry):
        rows = pl.ds(pl.multiple_of(i * BLOCK, BLOCK), BLOCK)
        x = nx_ref[rows, :]
        k = contract(x, wk_ref[...], 1, 0)
        ks[rows, :] = (k * cos_ref[rows, :] + swap(k) * sin_ref[rows, :]).astype(jnp.bfloat16)
        vs[rows, :] = contract(x, wv_ref[...], 1, 0).astype(jnp.bfloat16)
        dka[rows, :] = jnp.zeros((BLOCK, PAIR), jnp.float32)
        dva[rows, :] = jnp.zeros((BLOCK, PAIR), jnp.float32)
        return carry

    lax.fori_loop(0, total // BLOCK, project, 0)

    def query(i, carry):
        rows = pl.ds(pl.multiple_of(i * BLOCK, BLOCK), BLOCK)
        here = pl.ds(pl.multiple_of(i * BLOCK + W, BLOCK), BLOCK)
        q = contract(nx_ref[here, :], wq_ref[...], 1, 0)
        q = (q * cos_ref[here, :] + swap(q) * sin_ref[here, :]).astype(jnp.bfloat16)
        qs[rows, :] = q * jnp.bfloat16(SCORE_SCALE)
        return carry

    lax.fori_loop(0, own // BLOCK, query, 0)

    def visit(b, carry):
        rows = pl.ds(pl.multiple_of(b * BLOCK, BLOCK), BLOCK)
        here = pl.ds(pl.multiple_of(b * BLOCK + W, BLOCK), BLOCK)
        window = pl.ds(pl.multiple_of(b * BLOCK, BLOCK), SPAN)
        contexts, grads = [], []
        for h in range(2):
            mine = (lane // HD) == h
            kb = ks[window, :]
            vb = vs[window, :]
            qh = jnp.where(mine, qs[rows, :], jnp.bfloat16(0))
            gh = jnp.where(mine, do_ref[rows, :], jnp.bfloat16(0))
            s = contract(qh, kb, 1, 1) + bias[b]
            e = jnp.exp(s - jnp.max(s, axis=1, keepdims=True))
            w = e * (1.0 / jnp.sum(e, axis=1, keepdims=True))
            pb = w.astype(jnp.bfloat16)
            context = contract(pb, vb, 1, 0).astype(jnp.bfloat16)
            delta = jnp.sum(
                gh.astype(jnp.float32) * context.astype(jnp.float32), axis=1, keepdims=True
            )
            dp = contract(gh, vb, 1, 1)
            ds = (w * (dp - delta)).astype(jnp.bfloat16)
            contexts.append(context)
            grads.append(contract(ds, kb, 1, 0))
            dka[window, :] += contract(ds, qh, 0, 0)
            dva[window, :] += contract(pb, gh, 0, 0)
        first = lane < HD
        ctx_ref[rows, :] = jnp.where(first, contexts[0], contexts[1])
        g = jnp.where(first, grads[0], grads[1]) * SCORE_SCALE
        dq_ref[rows, :] = (g * cos_ref[here, :] - swap(g) * sin_ref[here, :]).astype(jnp.bfloat16)
        return carry

    lax.fori_loop(0, own // BLOCK, visit, 0)


def attention_kernel(
    core_ref, nx_ref, wq_ref, wk_ref, wv_ref, cos_ref, sin_ref, segq_ref, segk_ref, do_ref,
    ctx_ref, dq_ref, dk_ref, dv_ref,
    bias, qs, ks, vs, dka, dva,
):
    total = nx_ref.shape[0]
    lane = lax.broadcasted_iota(jnp.int32, (1, PAIR), 1)

    def swap(u):
        return swap_halves(u, lane)

    pair_attention(
        pl.program_id(0), nx_ref, wq_ref, wk_ref, wv_ref, cos_ref, sin_ref, segq_ref, segk_ref,
        do_ref, ctx_ref, dq_ref, bias, qs, ks, vs, dka, dva,
    )

    def finish(i, carry):
        rows = pl.ds(pl.multiple_of(i * BLOCK, BLOCK), BLOCK)
        g = dka[rows, :]
        dk_ref[rows, :] = (g * cos_ref[rows, :] - swap(g) * sin_ref[rows, :]).astype(jnp.bfloat16)
        dv_ref[rows, :] = dva[rows, :].astype(jnp.bfloat16)
        return carry

    lax.fori_loop(0, total // BLOCK, finish, 0)


def attention(core, nx, weights, cosine, sine, seg_q, seg_k, out_grads):
    total = nx.shape[0]
    own = total - W
    pairs = HALF // PAIR

    def whole(shape):
        return pl.BlockSpec(shape, lambda p, c: (0, 0))

    def columns(start):
        return pl.BlockSpec((D, PAIR), lambda p, c: (0, start + c[0] * pairs + p))

    def heads(rows):
        return pl.BlockSpec((rows, PAIR), lambda p, c: (0, p))

    return pl.pallas_call(
        attention_kernel,
        out_shape=[
            jax.ShapeDtypeStruct((own, HALF), jnp.bfloat16),
            jax.ShapeDtypeStruct((own, HALF), jnp.bfloat16),
            jax.ShapeDtypeStruct((total, HALF), jnp.bfloat16),
            jax.ShapeDtypeStruct((total, HALF), jnp.bfloat16),
        ],
        grid_spec=pltpu.PrefetchScalarGridSpec(
            num_scalar_prefetch=1,
            grid=(pairs,),
            in_specs=[
                whole((total, D)),
                columns(0),
                columns(2 * pairs),
                columns(4 * pairs),
                whole((total, PAIR)),
                whole((total, PAIR)),
                whole((own, 1)),
                whole((1, total)),
                heads(own),
            ],
            out_specs=[heads(own), heads(own), heads(total), heads(total)],
            scratch_shapes=[
                pltpu.VMEM((own // BLOCK, BLOCK, SPAN), jnp.float32),
                pltpu.VMEM((own, PAIR), jnp.bfloat16),
                pltpu.VMEM((total, PAIR), jnp.bfloat16),
                pltpu.VMEM((total, PAIR), jnp.bfloat16),
                pltpu.VMEM((total, PAIR), jnp.float32),
                pltpu.VMEM((total, PAIR), jnp.float32),
            ],
        ),
        compiler_params=pltpu.CompilerParams(vmem_limit_bytes=48 * 1024 * 1024),
        name="window_attention",
    )(core, nx, weights, weights, weights, cosine, sine, seg_q, seg_k, out_grads)


ROWS = 512
HALVES = 2
TABLE = HD // 2


def turn(angle):
    count = jnp.floor(angle * (2.0 / math.pi) + 0.5)
    r = angle - count * 1.5703125
    r = r - count * 4.837512969970703125e-4
    r = r - count * 7.54978995489188e-8
    z = r * r
    s = r + r * z * (-1.6666654611e-1 + z * (8.3321608736e-3 - z * 1.9515295891e-4))
    c = 1.0 - 0.5 * z + z * z * (4.166664568298827e-2 + z * (-1.388731625493765e-3 + z * 2.443315711809948e-5))
    quarter = count - 4.0 * jnp.floor(count * 0.25)
    odd = (quarter == 1.0) | (quarter == 3.0)
    sine = jnp.where(odd, c, s)
    cosine = jnp.where(odd, s, c)
    sine = jnp.where(quarter >= 2.0, -sine, sine)
    cosine = jnp.where((quarter == 1.0) | (quarter == 2.0), -cosine, cosine)
    return cosine, sine


def rotated(u, c, s):
    parts = []
    for h in range(2):
        a = u[h * HD : h * HD + TABLE]
        b = u[h * HD + TABLE : (h + 1) * HD]
        parts += [a * c - b * s, b * c + a * s]
    return jnp.concatenate(parts, axis=0)


class Unit:
    pass


def attend(entries, bias, qT, kT, vT, ks, vs, gT, ctxT, dqT, dkT, dvT):
    chunks = SPAN // BLOCK
    sub = lax.broadcasted_iota(jnp.int32, (PAIR, 1), 0)
    bf16, f32 = jnp.bfloat16, jnp.float32

    def unit(pair, slot, b, h):
        u = Unit()
        u.pair, u.slot, u.b, u.h = pair, slot, b, h
        u.cols = pl.ds(pl.multiple_of(b * BLOCK, BLOCK), BLOCK)
        u.head = slice(h * HD, (h + 1) * HD)
        u.mine = (sub // HD) == h
        return u

    def keys(u, c):
        return pl.ds(pl.multiple_of(u.b * BLOCK + c * BLOCK, BLOCK), BLOCK)

    def score(u, c):
        if c == 0:
            q = qT[u.slot, :, u.cols]
            u.q, u.qh, u.s = jnp.where(u.mine, q, bf16(0)), q[u.head], []
        s = contract(ks[u.slot, keys(u, c), :], u.q, 1, 0) + bias[u.b, c * BLOCK : (c + 1) * BLOCK, :]
        u.s.append(s)
        top = jnp.max(s.reshape(-1, 8, BLOCK), axis=0)
        u.m = top if c == 0 else jnp.maximum(u.m, top)
        if c == chunks - 1:
            u.m = jnp.max(u.m, axis=0, keepdims=True)

    def expand(u, c):
        if c == 0:
            u.e = []
        e = jnp.exp(u.s[c] - u.m)
        u.e.append(e)
        part = jnp.sum(e.reshape(-1, 8, BLOCK), axis=0)
        u.l = part if c == 0 else u.l + part
        if c == chunks - 1:
            u.inv = 1.0 / jnp.sum(u.l, axis=0, keepdims=True)

    def mix(u, c):
        if c == 0:
            u.w, u.p = [], []
        w = u.e[c] * u.inv
        u.w.append(w)
        u.p.append(w.astype(bf16))
        t = contract(vT[u.slot, u.head, keys(u, c)], u.p[c], 1, 0)
        u.ctx = t if c == 0 else u.ctx + t
        if c == chunks - 1:
            g = gT[pl.ds(pl.multiple_of(u.pair * PAIR, PAIR), PAIR), u.cols]
            u.g, u.gh = jnp.where(u.mine, g, bf16(0)), g[u.head]
            u.ctx = u.ctx.astype(bf16)
            ctxT[u.slot, u.head, u.cols] = u.ctx
            u.delta = jnp.sum(u.gh.astype(f32) * u.ctx.astype(f32), axis=0, keepdims=True)

    def slope(u, c):
        if c == 0:
            u.ds = []
        dp = contract(vs[u.slot, keys(u, c), :], u.g, 1, 0)
        u.ds.append((u.w[c] * (dp - u.delta)).astype(bf16))
        dvT[u.slot, u.head, keys(u, c)] += contract(u.gh, u.p[c], 1, 1)

    def back(u, c):
        t = contract(kT[u.slot, u.head, keys(u, c)], u.ds[c], 1, 0)
        u.dq = t if c == 0 else u.dq + t
        dkT[u.slot, u.head, keys(u, c)] += contract(u.qh, u.ds[c], 1, 1)
        if c == chunks - 1:
            dqT[u.slot, u.head, u.cols] = u.dq

    stages = [score, expand, mix, slope, back]
    units = [unit(*entry, h) for entry in entries for h in range(2)]
    for t in range(len(stages) + len(units) - 1):
        for c in range(chunks):
            for n, u in enumerate(units):
                if 0 <= t - n < len(stages):
                    stages[t - n](u, c)


def whole_kernel(
    x_ref, w_ref, pos_ref, seg_ref, g_ref, freq_ref,
    ctx_ref, ig_ref, pg_ref,
    nx, rms, wg, wpack, wT, meta, metag, gsend, gbuf, gT, cosT, sinT, segc, bias,
    qT, kT, vT, ks, vs, ctxT, dqT, dkT, dvT, dqb, dkvb, dtok,
    ctxs, ctxr, part, sums, joined, layered, decks, kept, give, got, ps, pr, fwd, later, ys, yr, ngo,
    w_send, w_recv, x_send, x_recv, m_send, m_recv, g_send, g_recv,
    side_send, side_recv, part_send, part_recv, deck_send, deck_recv, ctx_send, ctx_recv, n_send, n_recv,
    *, count, grad_scale,
):
    f32, bf16 = jnp.float32, jnp.bfloat16
    me = lax.axis_index("seq")
    core = lax.rem(me, 2)
    chip = lax.div(me, 2)
    chips = count // 2
    layers = count // 4
    partner = me + 1 - 2 * core
    side = lax.rem(chip, 2)
    layer = lax.div(chip, 2)
    share = D // count
    group = lax.axis_index("groups")
    mine_at = pl.multiple_of(core * ROWS, ROWS)
    other_at = pl.multiple_of((1 - core) * ROWS, ROWS)
    has_prev = chip > 0
    has_next = chip < chips - 1
    prev = lax.rem(me + count - 2, count)
    after = lax.rem(me + 2, count)

    def remote(source, target, send, recv, device, part_of=None):
        return pltpu.make_async_remote_copy(
            src_ref=source, dst_ref=target, send_sem=send, recv_sem=recv,
            device_id={"groups": group if part_of is None else part_of, "seq": device},
            device_id_type=pl.DeviceIdType.MESH,
        )

    def place(z, x, c):
        return (z * 2 + x) * 2 + c

    barrier = pltpu.get_barrier_semaphore()

    def greet(i, carry):
        pl.semaphore_signal(
            barrier, inc=1, device_id={"groups": group, "seq": lax.rem(me + 1 + i, count)},
            device_id_type=pl.DeviceIdType.MESH,
        )
        return carry

    lax.fori_loop(0, count - 1, greet, 0)
    pl.semaphore_signal(
        barrier, inc=1, device_id={"groups": 1 - group, "seq": me}, device_id_type=pl.DeviceIdType.MESH
    )

    for p in range(3):
        for h in range(2):
            wpack[p, h] = jnp.concatenate(
                [w_ref[:, t * D + h * HALF + p * PAIR : t * D + h * HALF + (p + 1) * PAIR] for t in range(3)],
                axis=1,
            )

    meta[0:1, :] = pos_ref[...]
    meta[1:2, :] = seg_ref[...]
    metag[2 + core] = meta[...]

    own_block = pl.ds(pl.multiple_of(me * share, share), share)
    for p in range(3):
        wg[p, own_block, :] = wpack[p, core]

    def block_of(device):
        return pl.ds(pl.multiple_of(device * share, share), share)

    def w_move(p, device, k, slot, to, part_of=None):
        rows = block_of(device)
        return remote(wg.at[p, rows, :], wg.at[p, rows, :], w_send.at[p, k], w_recv.at[p, slot], to, part_of)

    def hop_to(j):
        return lax.rem(layer + j, layers)

    def w_partner(p):
        return remote(
            wpack.at[p, 1 - core], wg.at[p, own_block, :], w_send.at[p, 0], w_recv.at[p, layer], partner
        )

    def w_near(p, j, c):
        return remote(
            wpack.at[p, c], wg.at[p, own_block, :], w_send.at[p, 2 * j - 1 + c], w_recv.at[p, layer],
            place(hop_to(j), side, c),
        )

    def w_cross(p, c):
        return remote(
            wpack.at[p, c], wg.at[p, own_block, :], w_send.at[p, 7 + c],
            w_recv.at[p, 2 * layers + layer], place(layer, 1 - side, c),
        )

    def w_around(p, j):
        return w_move(
            p, place(layer, 1 - side, group), 8 + j, 2 * layers + layer, place(hop_to(j), side, core)
        )

    def w_over_near(p, j):
        z = hop_to(j)
        return w_move(p, place(z, side, group), 11 + j, layers + z, me, 1 - group)

    def w_over_across(p, j):
        z = hop_to(j)
        return w_move(p, place(z, 1 - side, group), 15 + j, 3 * layers + z, me, 1 - group)

    def came(p, device, slot, part_of=None):
        w_move(p, device, 0, slot, partner, part_of).wait_recv()

    def loop(n, body):
        def step(i, carry):
            body(i)
            return carry

        lax.fori_loop(0, n, step, 0)

    def cross_weights(p):
        @pl.when(core == group)
        def _():
            for c in range(2):
                w_cross(p, c).start()

    def send_weights(p):
        w_partner(p).start()

        @pl.when(core == group)
        def _():
            for j in (2, 3, 1):
                for c in range(2):
                    w_near(p, j, c).start()

    def relay_first(p):
        came(p, place(layer, 1 - side, group), 2 * layers + layer)
        for j in (2, 3, 1):
            w_around(p, j).start()
        w_over_across(p, 0).start()

    def relay_near(p):
        for j in (1, 3, 2):
            came(p, place(hop_to(j), side, group), hop_to(j))
            w_over_near(p, j).start()

    def relay_across(p):
        for j in (1, 3, 2):
            came(p, place(hop_to(j), 1 - side, group), 2 * layers + hop_to(j))
            w_over_across(p, j).start()

    def await_weights(p):
        came(p, partner, layer)
        for j in range(1, layers):
            z = hop_to(j)
            came(p, place(z, side, 1 - group), layers + z)
        for j in range(layers):
            z = hop_to(j)
            came(p, place(z, 1 - side, 1 - group), 3 * layers + z)

    mine_rows = pl.ds(pl.multiple_of(W + mine_at, ROWS), ROWS)
    other_rows = pl.ds(pl.multiple_of(W + other_at, ROWS), ROWS)

    def chunk_rows(base, k):
        return pl.ds(pl.multiple_of(base + k * BLOCK, BLOCK), BLOCK)

    def x_swap():
        return remote(nx.at[mine_rows], nx.at[mine_rows], x_send.at[0], x_recv.at[0], partner)

    def x_swap_arrival():
        return remote(nx.at[other_rows], nx.at[other_rows], x_send.at[0], x_recv.at[0], partner)

    def x_next(k):
        n = 2 * k + core
        return remote(
            nx.at[chunk_rows(W, n)], nx.at[chunk_rows(0, n)], x_send.at[1 + k], x_recv.at[1 + k], after
        )

    def x_relay(k):
        rows = chunk_rows(0, 2 * k + core)
        return remote(nx.at[rows], nx.at[rows], x_send.at[3 + k], x_recv.at[3 + k], partner)

    def x_relay_arrival(k):
        rows = chunk_rows(0, 2 * k + 1 - core)
        return remote(nx.at[rows], nx.at[rows], x_send.at[3 + k], x_recv.at[3 + k], partner)

    def m_swap():
        return remote(metag.at[2 + core], metag.at[2 + core], m_send.at[0], m_recv.at[0], partner)

    def m_swap_arrival():
        return remote(metag.at[3 - core], metag.at[3 - core], m_send.at[0], m_recv.at[0], partner)

    def m_next(t):
        device = after - core + t
        return remote(meta, metag.at[core], m_send.at[1 + t], m_recv.at[1 + core], device)

    def m_prev_arrival(t):
        return remote(meta, metag.at[t], m_send.at[1 + t], m_recv.at[1 + t], prev)

    def g_swap():
        return remote(gsend, gbuf.at[pl.ds(mine_at, ROWS), :], g_send, g_recv, partner)

    def g_arrival():
        return remote(gsend, gbuf.at[pl.ds(other_at, ROWS), :], g_send, g_recv, partner)

    half_mine = pl.ds(pl.multiple_of(core * HALF, HALF), HALF)
    half_other = pl.ds(pl.multiple_of((1 - core) * HALF, HALF), HALF)
    gsend[...] = g_ref[:, half_other]
    gbuf[pl.ds(mine_at, ROWS), :] = g_ref[:, half_mine]

    def normalize(k):
        rows = pl.ds(pl.multiple_of(k * BLOCK, BLOCK), BLOCK)
        x = x_ref[rows, :].astype(f32)
        inv = lax.rsqrt(jnp.mean(x * x, axis=1, keepdims=True) + EPSILON)
        rms[rows, :] = inv
        nx[chunk_rows(W + mine_at, k), :] = (x * inv).astype(bf16)

    loop(2, normalize)

    pl.semaphore_wait(barrier, count)
    cross_weights(0)
    send_weights(0)
    cross_weights(1)
    cross_weights(2)
    m_swap().start()

    @pl.when(has_next)
    def _():
        m_next(0).start()
        m_next(1).start()

    x_swap().start()
    g_swap().start()

    relay_first(0)
    relay_near(0)
    x_swap_arrival().wait_recv()

    @pl.when(has_next)
    def _():
        x_next(1).start()
        x_next(0).start()

    send_weights(1)
    relay_first(1)
    relay_across(0)

    @pl.when(has_prev)
    def _():
        m_prev_arrival(0).wait_recv()
        m_prev_arrival(1).wait_recv()

    @pl.when(jnp.logical_not(has_prev))
    def _():
        row = lax.broadcasted_iota(jnp.int32, (8, ROWS), 0)
        gone = jnp.where(row == 1, -1, 0)
        metag[0] = gone
        metag[1] = gone
        nx[:W, :] = jnp.zeros((W, D), bf16)

    m_swap_arrival().wait_recv()
    g_arrival().wait_recv()

    for n in range(4):
        angle = metag[n][0:1, :].astype(f32) * freq_ref[:, 0:1]
        c, s = turn(angle)
        cosT[:, n * ROWS : (n + 1) * ROWS] = c
        sinT[:, n * ROWS : (n + 1) * ROWS] = s
        seg = metag[n][1:2, :].astype(f32)
        for j in range(ROWS // PAIR):
            flat = jnp.broadcast_to(seg[:, j * PAIR : (j + 1) * PAIR], (PAIR, PAIR))
            segc[n * ROWS + j * PAIR : n * ROWS + (j + 1) * PAIR, :] = jnp.transpose(flat)
    for n in range(2):
        gT[:, n * ROWS : (n + 1) * ROWS] = jnp.transpose(gbuf[n * ROWS : (n + 1) * ROWS, :])

    key = lax.broadcasted_iota(jnp.int32, (BLOCK, BLOCK), 0)
    query = lax.broadcasted_iota(jnp.int32, (BLOCK, BLOCK), 1)
    for b in range(W // BLOCK):
        at = b * BLOCK
        seg_q = metag[2 + at // ROWS][1:2, at % ROWS : at % ROWS + BLOCK].astype(f32)
        for c in range(SPAN // BLOCK):
            seg_k = segc[at + c * BLOCK : at + (c + 1) * BLOCK, :]
            same = jnp.concatenate([seg_k == seg_q[:, :PAIR], seg_k == seg_q[:, PAIR:]], axis=1)
            if c == 0:
                same = same & (key > query)
            if c == SPAN // BLOCK - 1:
                same = same & (key <= query)
            bias[b, c * BLOCK : (c + 1) * BLOCK, :] = jnp.where(same, 0.0, MASKED_SCORE)


    def table(n):
        cols = pl.ds(pl.multiple_of(n * BLOCK, BLOCK), BLOCK)
        return cols, cosT[:, cols], sinT[:, cols]

    def keep_kv(slot, cols, k, v):
        kT[slot, :, cols] = k
        vT[slot, :, cols] = v
        ks[slot, cols, :] = jnp.transpose(k)
        vs[slot, cols, :] = jnp.transpose(v)

    def project_before(slot, n):
        cols, c, s = table(n)
        kv = contract(wT[slot, PAIR:, :], nx[cols, :], 1, 1)
        keep_kv(slot, cols, rotated(kv[:PAIR], c, s).astype(bf16), kv[PAIR:].astype(bf16))

    def project_own(slot, i):
        cols, c, s = table(i + W // BLOCK)
        at = pl.ds(pl.multiple_of(i * BLOCK, BLOCK), BLOCK)
        qkv = contract(wT[slot], nx[cols, :], 1, 1)
        qT[slot, :, at] = rotated(qkv[:PAIR], c, s).astype(bf16) * bf16(SCORE_SCALE)
        k = rotated(qkv[PAIR : 2 * PAIR], c, s).astype(bf16)
        keep_kv(slot, cols, k, qkv[2 * PAIR :].astype(bf16))

    def finish_chunk(p, n):
        slot = lax.rem(p, 2)
        cols, c, s = table(n)
        k = rotated(dkT[slot, :, cols], c, -s).astype(bf16)
        v = dvT[slot, :, cols].astype(bf16)
        kv = jnp.concatenate([k, v], axis=0)
        dkvb[slot, :, cols] = kv
        dtok[p, cols, PAIR:] = jnp.transpose(kv)

    def finish_query(p, i):
        cols, c, s = table(i + W // BLOCK)
        at = pl.ds(pl.multiple_of(i * BLOCK, BLOCK), BLOCK)
        slot = lax.rem(p, 2)
        q = rotated(dqT[slot, :, at] * SCORE_SCALE, c, -s).astype(bf16)
        dqb[:, at] = q
        dtok[p, cols, :PAIR] = jnp.transpose(q)
        ctxs[p, at, :] = jnp.transpose(ctxT[slot, :, at])

    def ctx_copy(p):
        return remote(
            ctxs.at[p, pl.ds(other_at, ROWS), :], ctxr.at[p], ctx_send.at[p], ctx_recv.at[p], partner
        )

    deck = 2 * share

    def deck_rows(z, x):
        return pl.ds(pl.multiple_of((2 * z + x) * deck, deck), deck)

    def side_copy(p, z):
        return remote(
            part.at[p, deck_rows(z, 1 - side), :], sums.at[p, z], side_send.at[p, z], side_recv.at[p, z],
            place(layer, 1 - side, core),
        )

    def layer_copy(p, j):
        return remote(
            joined.at[p, j - 1], layered.at[p, j - 1], part_send.at[p, j - 1], part_recv.at[p, j - 1],
            place(hop_to(j), side, core),
        )

    def deck_copy(p):
        return remote(give.at[p], got.at[p], deck_send.at[p], deck_recv.at[p], partner)

    def both_sides(p, z):
        side_copy(p, z).wait_recv()
        return part[p, deck_rows(z, side), :].astype(f32) + sums[p, z].astype(f32)

    def join(p):
        for j in (2, 3, 1):
            joined[p, j - 1] = both_sides(p, hop_to(j)).astype(bf16)
            layer_copy(p, j).start()

    def share_out(p):
        total = both_sides(p, layer)
        for j in range(1, layers):
            layer_copy(p, j).wait_recv()
            total = total + layered[p, j - 1].astype(f32)
        decks[...] = total

        def rows(c):
            return decks[pl.ds(pl.multiple_of(c * share, share), share), :]

        give[p] = rows(1 - core).astype(bf16)
        deck_copy(p).start()
        kept[p] = rows(core)

    def collect(p):
        deck_copy(p).wait_recv()
        even = kept[p]
        odd = got[p].astype(f32)
        for t in range(3):
            at = t * D + p * PAIR
            a = pl.ds(pl.multiple_of(at + core * HALF, PAIR), PAIR)
            b = pl.ds(pl.multiple_of(at + (1 - core) * HALF, PAIR), PAIR)
            pg_ref[:, a] = even[:, t * PAIR : (t + 1) * PAIR] * grad_scale
            pg_ref[:, b] = odd[:, t * PAIR : (t + 1) * PAIR] * grad_scale

    def n_swap(k):
        return remote(ps.at[k], pr.at[k], n_send.at[k], n_recv.at[k], partner)

    def n_back(k):
        return remote(fwd.at[k], later.at[k], n_send.at[2 + k], n_recv.at[2 + k], prev)

    def n_own():
        return remote(ys, yr, n_send.at[4], n_recv.at[4], partner)

    def give_before(half, k):
        rows = chunk_rows(half * ROWS, k)
        mine = sum(contract(dtok[p, rows, PAIR:], wg[p, :, PAIR:], 1, 1) for p in range(3))

        @pl.when(core != half)
        def _():
            ps[k] = mine.astype(bf16)
            n_swap(k).start()

        @pl.when(core == half)
        def _():
            ngo[pl.ds(pl.multiple_of(k * BLOCK, BLOCK), BLOCK), :] = mine

    def pass_before(half, k):
        @pl.when(core == half)
        def _():
            n_swap(k).wait_recv()
            mine = ngo[pl.ds(pl.multiple_of(k * BLOCK, BLOCK), BLOCK), :]
            fwd[k] = (mine + pr[k].astype(f32)).astype(bf16)

            @pl.when(has_prev)
            def _():
                n_back(k).start()

    def own_grad(at, k):
        rows = chunk_rows(W + at, k)
        return sum(contract(dtok[p, rows, :], wg[p], 1, 1) for p in range(3))

    def begin(p, slot):
        await_weights(p)
        wT[slot] = jnp.transpose(wg[p])
        loop(4, lambda i: project_own(slot, i))
        dkT[slot] = jnp.zeros((PAIR, 2 * W), f32)
        dvT[slot] = jnp.zeros((PAIR, 2 * W), f32)

    def project_gradient(p):
        loop(4, lambda n: finish_chunk(p, n + 4))
        loop(4, lambda n: finish_query(p, n))
        kv = contract(dkvb[lax.rem(p, 2)], nx[...], 1, 0)
        q = contract(dqb[...], nx[W:, :], 1, 0)
        part[p, :, :PAIR] = jnp.transpose(q.astype(bf16))
        part[p, :, PAIR:] = jnp.transpose(kv.astype(bf16))

    def send_gradient(p):
        for j in (2, 3, 1, 0):
            side_copy(p, hop_to(j)).start()
        ctx_copy(p).start()

    def relay_both(p):
        relay_near(p)
        relay_across(p)

    def step(t):
        p = jnp.where(t < 2, 0, jnp.where(t == 3, 2, 1))
        slot = lax.rem(p, 2)
        half = jnp.where((t == 0) | (t == 4), 1, 0)

        @pl.when((t == 0) | (t == 2) | (t == 3))
        def _():
            begin(p, slot)

        @pl.when((t < 2) & has_prev)
        def _():
            x_next(half).wait_recv()
            x_relay(half).start()
            x_relay_arrival(half).wait_recv()

        @pl.when(t < 2)
        def _():
            loop(2, lambda k: project_before(slot, half * 2 + k))

        @pl.when((t == 2) | (t == 3))
        def _():
            loop(4, lambda k: project_before(slot, k))

        @pl.when(((t == 1) & (side == 0)) | (t == 2))
        def _():
            relay_both(t)

        attend(
            [(p, slot, 2 * half), (p, slot, 2 * half + 1)],
            bias, qT, kT, vT, ks, vs, gT, ctxT, dqT, dkT, dvT,
        )

        @pl.when(t == 0)
        def _():
            relay_first(2)
            send_weights(2)

        @pl.when((t == 1) & (side == 1))
        def _():
            relay_both(1)

        @pl.when(t == 1)
        def _():
            loop(2, lambda n: finish_chunk(p, n))

        @pl.when((t == 1) | (t == 4))
        def _():
            loop(2, lambda n: finish_chunk(p, n + 2))
            project_gradient(p)
            send_gradient(p)

        @pl.when(t == 2)
        def _():
            join(0)

        @pl.when(t == 3)
        def _():
            def finished(k):
                finish_chunk(1, k)
                finish_chunk(2, k)
                give_before(0, k)

            loop(2, finished)
            share_out(0)
            loop(2, lambda k: pass_before(0, k))

    loop(5, step)

    def last_step(k):
        attend([(2, 0, k + 2)], bias, qT, kT, vT, ks, vs, gT, ctxT, dqT, dkT, dvT)
        finish_chunk(2, k + 2)
        give_before(1, k)

        pass_before(1, k)

    loop(2, last_step)
    project_gradient(2)
    send_gradient(2)

    def give_own(k):
        ys[pl.ds(pl.multiple_of(k * BLOCK, BLOCK), BLOCK), :] = own_grad(other_at, k).astype(bf16)

    loop(2, give_own)
    n_own().start()

    def keep_own(k):
        ngo[pl.ds(pl.multiple_of(k * BLOCK, BLOCK), BLOCK), :] = own_grad(mine_at, k)

    loop(2, keep_own)
    join(1)
    join(2)

    for p in range(3):
        ctx_copy(p).wait()
        mine_cols = pl.ds(pl.multiple_of(core * HALF + p * PAIR, PAIR), PAIR)
        other_cols = pl.ds(pl.multiple_of((1 - core) * HALF + p * PAIR, PAIR), PAIR)
        ctx_ref[:, mine_cols] = ctxs[p, pl.ds(mine_at, ROWS), :]
        ctx_ref[:, other_cols] = ctxr[p]

    collect(0)
    share_out(1)
    share_out(2)
    collect(1)
    n_own().wait()

    @pl.when(has_next)
    def _():
        n_back(0).wait_recv()
        n_back(1).wait_recv()

    @pl.when(jnp.logical_not(has_next))
    def _():
        later[...] = jnp.zeros_like(later)

    def finish(k):
        rows = pl.ds(pl.multiple_of(k * BLOCK, BLOCK), BLOCK)
        ng = ngo[rows, :] + yr[rows, :].astype(f32) + later[k].astype(f32)
        inv = rms[rows, :]
        scaled = x_ref[rows, :].astype(f32) * inv
        ig_ref[rows, :] = (
            inv * (ng - scaled * jnp.mean(ng * scaled, axis=1, keepdims=True))
        ).astype(bf16)

    loop(2, finish)
    collect(2)

    for p in range(3):
        @pl.when(core == group)
        def _():
            for c in range(2):
                w_cross(p, c).wait_send()

                for j in range(1, layers):
                    w_near(p, j, c).wait_send()

        w_partner(p).wait_send()
        w_over_across(p, 0).wait_send()
        for j in range(1, layers):
            w_around(p, j).wait_send()
            w_over_near(p, j).wait_send()
            w_over_across(p, j).wait_send()
            layer_copy(p, j).wait_send()
        for z in range(layers):
            side_copy(p, z).wait_send()
        deck_copy(p).wait_send()
    m_swap().wait_send()
    x_swap().wait_send()
    g_swap().wait_send()

    @pl.when(has_next)
    def _():
        for k in range(2):
            m_next(k).wait_send()
            x_next(k).wait_send()

    @pl.when(has_prev)
    def _():
        for k in range(2):
            x_relay(k).wait_send()
            n_back(k).wait_send()

    for k in range(2):
        n_swap(k).wait_send()


def whole(count, grad_scale, x, weights, positions, segments, out_grads):
    share = D // count
    bf16, f32 = jnp.bfloat16, jnp.float32
    total = 2 * W
    vmem = pl.BlockSpec(memory_space=pltpu.VMEM)
    frequency = np.exp(np.float32(-math.log(10000.0)) * np.arange(TABLE, dtype=np.float32) / np.float32(TABLE))
    frequency = np.broadcast_to(frequency.astype(np.float32)[:, None], (TABLE, PAIR))
    dma = pltpu.SemaphoreType.DMA
    layers = count // 4
    return pl.pallas_call(
        functools.partial(whole_kernel, count=count, grad_scale=grad_scale),
        out_shape=[
            jax.ShapeDtypeStruct((ROWS, D), bf16),
            jax.ShapeDtypeStruct((ROWS, D), bf16),
            jax.ShapeDtypeStruct((share, 3 * D), f32),
        ],
        in_specs=[vmem] * 6,
        out_specs=[vmem] * 3,
        scratch_shapes=[
            pltpu.VMEM((total, D), bf16),
            pltpu.VMEM((ROWS, 1), f32),
            pltpu.VMEM((3, D, 3 * PAIR), bf16),
            pltpu.VMEM((3, 2, share, 3 * PAIR), bf16),
            pltpu.VMEM((2, 3 * PAIR, D), bf16),
            pltpu.VMEM((8, ROWS), jnp.int32),
            pltpu.VMEM((4, 8, ROWS), jnp.int32),
            pltpu.VMEM((ROWS, HALF), bf16),
            pltpu.VMEM((W, HALF), bf16),
            pltpu.VMEM((HALF, W), bf16),
            pltpu.VMEM((TABLE, total), f32),
            pltpu.VMEM((TABLE, total), f32),
            pltpu.VMEM((total, PAIR), f32),
            pltpu.VMEM((W // BLOCK, SPAN, BLOCK), f32),
            pltpu.VMEM((2, PAIR, W), bf16),
            pltpu.VMEM((2, PAIR, total), bf16),
            pltpu.VMEM((2, PAIR, total), bf16),
            pltpu.VMEM((2, total, PAIR), bf16),
            pltpu.VMEM((2, total, PAIR), bf16),
            pltpu.VMEM((2, PAIR, W), bf16),
            pltpu.VMEM((2, PAIR, W), f32),
            pltpu.VMEM((2, PAIR, total), f32),
            pltpu.VMEM((2, PAIR, total), f32),
            pltpu.VMEM((PAIR, W), bf16),
            pltpu.VMEM((2, 2 * PAIR, total), bf16),
            pltpu.VMEM((3, total, 3 * PAIR), bf16),
            pltpu.VMEM((3, W, PAIR), bf16),
            pltpu.VMEM((3, ROWS, PAIR), bf16),
            pltpu.VMEM((3, D, 3 * PAIR), bf16),
            pltpu.VMEM((3, layers, 2 * share, 3 * PAIR), bf16),
            pltpu.VMEM((3, layers - 1, 2 * share, 3 * PAIR), bf16),
            pltpu.VMEM((3, layers - 1, 2 * share, 3 * PAIR), bf16),
            pltpu.VMEM((2 * share, 3 * PAIR), f32),
            pltpu.VMEM((3, share, 3 * PAIR), f32),
            pltpu.VMEM((3, share, 3 * PAIR), bf16),
            pltpu.VMEM((3, share, 3 * PAIR), bf16),
            pltpu.VMEM((2, BLOCK, D), bf16),
            pltpu.VMEM((2, BLOCK, D), bf16),
            pltpu.VMEM((2, BLOCK, D), bf16),
            pltpu.VMEM((2, BLOCK, D), bf16),
            pltpu.VMEM((ROWS, D), bf16),
            pltpu.VMEM((ROWS, D), bf16),
            pltpu.VMEM((ROWS, D), f32),
            dma((3, 15 + layers)), dma((3, 4 * layers)),
            dma((5,)), dma((5,)),
            dma((3,)), dma((3,)),
            dma, dma,
            dma((3, layers)), dma((3, layers)),
            dma((3, layers - 1)), dma((3, layers - 1)),
            dma((3,)), dma((3,)),
            dma((3,)), dma((3,)),
            dma((5,)), dma((5,)),
        ],
        compiler_params=pltpu.CompilerParams(
            vmem_limit_bytes=60 * 1024 * 1024, collective_id=0, has_side_effects=True
        ),
        name="whole_sublayer",
    )(x, weights, positions, segments, out_grads, frequency)


def swapped(value):
    count = lax.axis_size("seq")
    return lax.ppermute(value, "seq", [(s, s ^ 1) for s in range(count)])


def chip_shifted(value, steps):
    count = lax.axis_size("seq")
    pairs = [(s, s + 2 * steps) for s in range(count) if 0 <= s + 2 * steps < count]
    return lax.ppermute(value, "seq", pairs)


def ordered(core, mine, other, axis=0):
    first = jnp.where(core == 0, mine, other)
    second = jnp.where(core == 0, other, mine)
    return jnp.concatenate([first, second], axis=axis)


def local(inputs, projection, positions, segments, context_grad):
    row_count = inputs.shape[0]
    device_count = lax.axis_size("seq")
    chips = device_count // 2
    device_index = lax.axis_index("seq")
    core = device_index % 2
    chip = device_index // 2
    assert 2 * row_count == W
    grad_scale = (row_count * device_count) ** (-0.5)

    if device_count == 16 and lax.axis_size("groups") == 2:
        return tuple(
            whole(
                device_count, grad_scale, inputs, projection, positions[None, :], segments[None, :],
                context_grad,
            )
        )

    weights = lax.all_gather(projection, "seq", axis=0, tiled=True)

    meta = jnp.stack([positions, segments], axis=0)
    x_before = chip_shifted(inputs, 1)
    meta_before = chip_shifted(meta, 1)
    x_other = swapped(inputs)
    meta_other = swapped(meta)
    x_before_other = swapped(x_before)
    meta_before_other = swapped(meta_before)
    grad_mine = lax.dynamic_slice_in_dim(context_grad, core * HALF, HALF, 1)
    grad_sent = lax.dynamic_slice_in_dim(context_grad, (1 - core) * HALF, HALF, 1)
    grad_other = swapped(grad_sent)
    out_grads = ordered(core, grad_mine, grad_other)

    x_all = jnp.concatenate(
        [ordered(core, x_before, x_before_other), ordered(core, inputs, x_other)], axis=0
    ).astype(jnp.float32)
    nx = (
        x_all * lax.rsqrt(jnp.mean(x_all * x_all, axis=1, keepdims=True) + EPSILON)
    ).astype(jnp.bfloat16)
    meta_all = jnp.concatenate(
        [ordered(core, meta_before, meta_before_other, 1), ordered(core, meta, meta_other, 1)],
        axis=1,
    )
    half_size = HD // 2
    frequency = jnp.exp(-math.log(10000.0) * jnp.arange(half_size, dtype=jnp.float32) / half_size)
    angle = meta_all[0].astype(jnp.float32)[:, None] * frequency[None, :]
    c, s = jnp.cos(angle), jnp.sin(angle)
    cosine = jnp.concatenate([c, c, c, c], axis=1)
    sine = jnp.concatenate([-s, s, -s, s], axis=1)
    seg_all = meta_all[1]
    outside = (jnp.arange(seg_all.shape[0]) < W) & (chip == 0)
    seg_k = jnp.where(outside, -1, seg_all)[None, :]
    seg_q = seg_all[W:][:, None]

    x_float = inputs.astype(jnp.float32)
    inv_rms = lax.rsqrt(jnp.mean(x_float * x_float, axis=1, keepdims=True) + EPSILON)
    scaled = x_float * inv_rms

    context_heads, dq, dk, dv = attention(
        core.astype(jnp.int32)[None], nx, weights, cosine, sine, seg_q, seg_k, out_grads
    )

    mine_at = core * row_count
    other_at = (1 - core) * row_count
    context_mine = lax.dynamic_slice_in_dim(context_heads, mine_at, row_count, 0)
    context_other = swapped(lax.dynamic_slice_in_dim(context_heads, other_at, row_count, 0))
    context = ordered(core, context_mine, context_other, 1)

    w_q, w_k, w_v = [
        lax.dynamic_slice_in_dim(weights, t * D + core * HALF, HALF, 1) for t in range(3)
    ]
    dkv = jnp.concatenate([dk, dv], axis=1)
    w_kv = jnp.concatenate([w_k, w_v], axis=1)
    ng_kv = contract(dkv, w_kv, 1, 1)
    ng_q = contract(dq, w_q, 1, 1)
    ng_before = ng_kv[:W]
    ng_own = ng_kv[W:] + ng_q
    send_before = lax.dynamic_slice_in_dim(ng_before, other_at, row_count, 0).astype(jnp.bfloat16)
    keep_before = lax.dynamic_slice_in_dim(ng_before, mine_at, row_count, 0)
    before = keep_before + swapped(send_before).astype(jnp.float32)
    later = chip_shifted(before.astype(jnp.bfloat16), -1)
    send_own = lax.dynamic_slice_in_dim(ng_own, other_at, row_count, 0).astype(jnp.bfloat16)
    keep_own = lax.dynamic_slice_in_dim(ng_own, mine_at, row_count, 0)
    normed_grad = (
        keep_own + swapped(send_own).astype(jnp.float32) + later.astype(jnp.float32)
    )
    input_grad = (
        inv_rms * (normed_grad - scaled * jnp.mean(normed_grad * scaled, axis=1, keepdims=True))
    ).astype(jnp.bfloat16)

    pg_kv = contract(nx, dkv, 0, 0)
    pg_q = contract(nx[W:], dq, 0, 0)
    pg = jnp.concatenate([pg_q, pg_kv], axis=1).astype(jnp.bfloat16)
    groups = [[2 * i + k for i in range(chips)] for k in range(2)]
    summed = lax.psum_scatter(
        pg, "seq", scatter_dimension=0, axis_index_groups=groups, tiled=True
    ).astype(jnp.float32)
    rows = summed.shape[0] // 2
    keep = lax.dynamic_slice_in_dim(summed, core * rows, rows, 0)
    other = swapped(lax.dynamic_slice_in_dim(summed, (1 - core) * rows, rows, 0).astype(jnp.bfloat16))
    other = other.astype(jnp.float32)
    parts = []
    for t in range(3):
        cols = slice(t * HALF, (t + 1) * HALF)
        parts.append(ordered(core, keep[:, cols], other[:, cols], 1))
    projection_grad = jnp.concatenate(parts, axis=1) * grad_scale
    return (context, input_grad, projection_grad)


def solution(mesh):
    in_specs = (
        P(("groups", "seq"), None),
        P("seq", None),
        P(("groups", "seq")),
        P(("groups", "seq")),
        P(("groups", "seq"), None),
    )
    out_specs = (P(("groups", "seq"), None), P(("groups", "seq"), None), P(("groups", "seq"), None))
    return jax.shard_map(local, mesh=mesh, in_specs=in_specs, out_specs=out_specs, check_vma=False)
```

```python
import functools
import math

import jax
import jax.numpy as jnp
import numpy as np
from jax import lax
from jax.experimental import pallas as pl
from jax.experimental.pallas import tpu as pltpu
from jax.sharding import PartitionSpec as P

D = 768
H = 12
HD = 64
W = 1024
EPSILON = 1e-05
SCORE_SCALE = 0.125
MASKED_SCORE = -1e30
BLOCK = 256
SPAN = BLOCK + W
PAIR = 2 * HD
HALF = D // 2


def contract(a, b, da, db):
    return lax.dot_general(a, b, (((da,), (db,)), ((), ())), preferred_element_type=jnp.float32)


def swap_halves(u, lane):
    low = (lane % HD) < HD // 2
    return jnp.where(low, pltpu.roll(u, PAIR - HD // 2, 1), pltpu.roll(u, HD // 2, 1))


def pair_attention(
    p, nx_ref, wq_ref, wk_ref, wv_ref, cos_ref, sin_ref, segq_ref, segk_ref, do_ref,
    ctx_ref, dq_ref,
    bias, qs, ks, vs, dka, dva,
):
    own = ctx_ref.shape[0]
    total = nx_ref.shape[0]
    lane = lax.broadcasted_iota(jnp.int32, (1, PAIR), 1)

    def swap(u):
        return swap_halves(u, lane)

    @pl.when(p == 0)
    def _():
        row = lax.broadcasted_iota(jnp.int32, (BLOCK, SPAN), 0)
        col = lax.broadcasted_iota(jnp.int32, (BLOCK, SPAN), 1)
        near = (col > row) & (col <= row + W)
        for b in range(own // BLOCK):
            same = segq_ref[b * BLOCK : (b + 1) * BLOCK, :] == segk_ref[:, b * BLOCK : b * BLOCK + SPAN]
            bias[b] = jnp.where(near & same, 0.0, MASKED_SCORE)

    def project(i, carry):
        rows = pl.ds(pl.multiple_of(i * BLOCK, BLOCK), BLOCK)
        x = nx_ref[rows, :]
        k = contract(x, wk_ref[...], 1, 0)
        ks[rows, :] = (k * cos_ref[rows, :] + swap(k) * sin_ref[rows, :]).astype(jnp.bfloat16)
        vs[rows, :] = contract(x, wv_ref[...], 1, 0).astype(jnp.bfloat16)
        dka[rows, :] = jnp.zeros((BLOCK, PAIR), jnp.float32)
        dva[rows, :] = jnp.zeros((BLOCK, PAIR), jnp.float32)
        return carry

    lax.fori_loop(0, total // BLOCK, project, 0)

    def query(i, carry):
        rows = pl.ds(pl.multiple_of(i * BLOCK, BLOCK), BLOCK)
        here = pl.ds(pl.multiple_of(i * BLOCK + W, BLOCK), BLOCK)
        q = contract(nx_ref[here, :], wq_ref[...], 1, 0)
        q = (q * cos_ref[here, :] + swap(q) * sin_ref[here, :]).astype(jnp.bfloat16)
        qs[rows, :] = q * jnp.bfloat16(SCORE_SCALE)
        return carry

    lax.fori_loop(0, own // BLOCK, query, 0)

    def visit(b, carry):
        rows = pl.ds(pl.multiple_of(b * BLOCK, BLOCK), BLOCK)
        here = pl.ds(pl.multiple_of(b * BLOCK + W, BLOCK), BLOCK)
        window = pl.ds(pl.multiple_of(b * BLOCK, BLOCK), SPAN)
        contexts, grads = [], []
        for h in range(2):
            mine = (lane // HD) == h
            kb = ks[window, :]
            vb = vs[window, :]
            qh = jnp.where(mine, qs[rows, :], jnp.bfloat16(0))
            gh = jnp.where(mine, do_ref[rows, :], jnp.bfloat16(0))
            s = contract(qh, kb, 1, 1) + bias[b]
            e = jnp.exp(s - jnp.max(s, axis=1, keepdims=True))
            w = e * (1.0 / jnp.sum(e, axis=1, keepdims=True))
            pb = w.astype(jnp.bfloat16)
            context = contract(pb, vb, 1, 0).astype(jnp.bfloat16)
            delta = jnp.sum(
                gh.astype(jnp.float32) * context.astype(jnp.float32), axis=1, keepdims=True
            )
            dp = contract(gh, vb, 1, 1)
            ds = (w * (dp - delta)).astype(jnp.bfloat16)
            contexts.append(context)
            grads.append(contract(ds, kb, 1, 0))
            dka[window, :] += contract(ds, qh, 0, 0)
            dva[window, :] += contract(pb, gh, 0, 0)
        first = lane < HD
        ctx_ref[rows, :] = jnp.where(first, contexts[0], contexts[1])
        g = jnp.where(first, grads[0], grads[1]) * SCORE_SCALE
        dq_ref[rows, :] = (g * cos_ref[here, :] - swap(g) * sin_ref[here, :]).astype(jnp.bfloat16)
        return carry

    lax.fori_loop(0, own // BLOCK, visit, 0)


def attention_kernel(
    core_ref, nx_ref, wq_ref, wk_ref, wv_ref, cos_ref, sin_ref, segq_ref, segk_ref, do_ref,
    ctx_ref, dq_ref, dk_ref, dv_ref,
    bias, qs, ks, vs, dka, dva,
):
    total = nx_ref.shape[0]
    lane = lax.broadcasted_iota(jnp.int32, (1, PAIR), 1)

    def swap(u):
        return swap_halves(u, lane)

    pair_attention(
        pl.program_id(0), nx_ref, wq_ref, wk_ref, wv_ref, cos_ref, sin_ref, segq_ref, segk_ref,
        do_ref, ctx_ref, dq_ref, bias, qs, ks, vs, dka, dva,
    )

    def finish(i, carry):
        rows = pl.ds(pl.multiple_of(i * BLOCK, BLOCK), BLOCK)
        g = dka[rows, :]
        dk_ref[rows, :] = (g * cos_ref[rows, :] - swap(g) * sin_ref[rows, :]).astype(jnp.bfloat16)
        dv_ref[rows, :] = dva[rows, :].astype(jnp.bfloat16)
        return carry

    lax.fori_loop(0, total // BLOCK, finish, 0)


def attention(core, nx, weights, cosine, sine, seg_q, seg_k, out_grads):
    total = nx.shape[0]
    own = total - W
    pairs = HALF // PAIR

    def whole(shape):
        return pl.BlockSpec(shape, lambda p, c: (0, 0))

    def columns(start):
        return pl.BlockSpec((D, PAIR), lambda p, c: (0, start + c[0] * pairs + p))

    def heads(rows):
        return pl.BlockSpec((rows, PAIR), lambda p, c: (0, p))

    return pl.pallas_call(
        attention_kernel,
        out_shape=[
            jax.ShapeDtypeStruct((own, HALF), jnp.bfloat16),
            jax.ShapeDtypeStruct((own, HALF), jnp.bfloat16),
            jax.ShapeDtypeStruct((total, HALF), jnp.bfloat16),
            jax.ShapeDtypeStruct((total, HALF), jnp.bfloat16),
        ],
        grid_spec=pltpu.PrefetchScalarGridSpec(
            num_scalar_prefetch=1,
            grid=(pairs,),
            in_specs=[
                whole((total, D)),
                columns(0),
                columns(2 * pairs),
                columns(4 * pairs),
                whole((total, PAIR)),
                whole((total, PAIR)),
                whole((own, 1)),
                whole((1, total)),
                heads(own),
            ],
            out_specs=[heads(own), heads(own), heads(total), heads(total)],
            scratch_shapes=[
                pltpu.VMEM((own // BLOCK, BLOCK, SPAN), jnp.float32),
                pltpu.VMEM((own, PAIR), jnp.bfloat16),
                pltpu.VMEM((total, PAIR), jnp.bfloat16),
                pltpu.VMEM((total, PAIR), jnp.bfloat16),
                pltpu.VMEM((total, PAIR), jnp.float32),
                pltpu.VMEM((total, PAIR), jnp.float32),
            ],
        ),
        compiler_params=pltpu.CompilerParams(vmem_limit_bytes=48 * 1024 * 1024),
        name="window_attention",
    )(core, nx, weights, weights, weights, cosine, sine, seg_q, seg_k, out_grads)


ROWS = 512
HALVES = 2
TABLE = HD // 2


def turn(angle):
    count = jnp.floor(angle * (2.0 / math.pi) + 0.5)
    r = angle - count * 1.5703125
    r = r - count * 4.837512969970703125e-4
    r = r - count * 7.54978995489188e-8
    z = r * r
    s = r + r * z * (-1.6666654611e-1 + z * (8.3321608736e-3 - z * 1.9515295891e-4))
    c = 1.0 - 0.5 * z + z * z * (4.166664568298827e-2 + z * (-1.388731625493765e-3 + z * 2.443315711809948e-5))
    quarter = count - 4.0 * jnp.floor(count * 0.25)
    odd = (quarter == 1.0) | (quarter == 3.0)
    sine = jnp.where(odd, c, s)
    cosine = jnp.where(odd, s, c)
    sine = jnp.where(quarter >= 2.0, -sine, sine)
    cosine = jnp.where((quarter == 1.0) | (quarter == 2.0), -cosine, cosine)
    return cosine, sine


def rotated(u, c, s):
    parts = []
    for h in range(2):
        a = u[h * HD : h * HD + TABLE]
        b = u[h * HD + TABLE : (h + 1) * HD]
        parts += [a * c - b * s, b * c + a * s]
    return jnp.concatenate(parts, axis=0)


def frequencies():
    steps = np.arange(TABLE, dtype=np.float32) / np.float32(TABLE)
    return [float(f) for f in np.exp(np.float32(-math.log(10000.0)) * steps).astype(np.float32)]


class Unit:
    pass


def attend(entries, bias, qT, kT, vT, ks, vs, gT, ctxT, dqT, dkT, dvT):
    chunks = SPAN // BLOCK
    sub = lax.broadcasted_iota(jnp.int32, (PAIR, 1), 0)
    bf16, f32 = jnp.bfloat16, jnp.float32

    def unit(pair, slot, b, h):
        u = Unit()
        u.pair, u.slot, u.b, u.h = pair, slot, b, h
        u.cols = pl.ds(pl.multiple_of(b * BLOCK, BLOCK), BLOCK)
        u.head = slice(h * HD, (h + 1) * HD)
        u.mine = (sub // HD) == h
        return u

    def keys(u, c):
        return pl.ds(pl.multiple_of(u.b * BLOCK + c * BLOCK, BLOCK), BLOCK)

    def score(u, c):
        if c == 0:
            q = qT[u.slot, :, u.cols]
            u.q, u.qh, u.s = jnp.where(u.mine, q, bf16(0)), q[u.head], []
        s = contract(ks[u.slot, keys(u, c), :], u.q, 1, 0) + bias[u.b, c * BLOCK : (c + 1) * BLOCK, :]
        u.s.append(s)
        top = jnp.max(s.reshape(-1, 8, BLOCK), axis=0)
        u.m = top if c == 0 else jnp.maximum(u.m, top)
        if c == chunks - 1:
            u.m = jnp.max(u.m, axis=0, keepdims=True)

    def expand(u, c):
        if c == 0:
            u.e = []
        e = jnp.exp(u.s[c] - u.m)
        u.e.append(e)
        part = jnp.sum(e.reshape(-1, 8, BLOCK), axis=0)
        u.l = part if c == 0 else u.l + part
        if c == chunks - 1:
            u.inv = 1.0 / jnp.sum(u.l, axis=0, keepdims=True)

    def mix(u, c):
        if c == 0:
            u.w, u.p = [], []
        w = u.e[c] * u.inv
        u.w.append(w)
        u.p.append(w.astype(bf16))
        t = contract(vT[u.slot, u.head, keys(u, c)], u.p[c], 1, 0)
        u.ctx = t if c == 0 else u.ctx + t
        if c == chunks - 1:
            g = gT[pl.ds(pl.multiple_of(u.pair * PAIR, PAIR), PAIR), u.cols]
            u.g, u.gh = jnp.where(u.mine, g, bf16(0)), g[u.head]
            u.ctx = u.ctx.astype(bf16)
            ctxT[u.slot, u.head, u.cols] = u.ctx
            u.delta = jnp.sum(u.gh.astype(f32) * u.ctx.astype(f32), axis=0, keepdims=True)

    def slope(u, c):
        if c == 0:
            u.ds = []
        dp = contract(vs[u.slot, keys(u, c), :], u.g, 1, 0)
        u.ds.append((u.w[c] * (dp - u.delta)).astype(bf16))
        dvT[u.slot, u.head, keys(u, c)] += contract(u.gh, u.p[c], 1, 1)

    def back(u, c):
        t = contract(kT[u.slot, u.head, keys(u, c)], u.ds[c], 1, 0)
        u.dq = t if c == 0 else u.dq + t
        dkT[u.slot, u.head, keys(u, c)] += contract(u.qh, u.ds[c], 1, 1)
        if c == chunks - 1:
            dqT[u.slot, u.head, u.cols] = u.dq

    stages = [score, expand, mix, slope, back]
    units = [unit(*entry, h) for entry in entries for h in range(2)]
    for t in range(len(stages) + len(units) - 1):
        for c in range(chunks):
            for n, u in enumerate(units):
                if 0 <= t - n < len(stages):
                    stages[t - n](u, c)


def whole_kernel(
    x_ref, w_ref, pos_ref, seg_ref, g_ref,
    ctx_out, ig_out, pg_out,
    ctx_ref, ig_ref, pg_ref, nx, rms, wg, wpack, wT, meta, metag, gsend, gbuf, gT, cosT, sinT, segc, bias,
    qT, kT, vT, ks, vs, ctxT, dqT, dkT, dvT, dqb, dkvb, dtok,
    ctxs, ctxr, part, sums, joined, layered, decks, kept, give, got, ps, pr, fwd, later, ys, yr, ngo,
    w_send, w_recv, x_send, x_recv, m_send, m_recv, g_send, g_recv,
    side_send, side_recv, part_send, part_recv, deck_send, deck_recv, ctx_send, ctx_recv, n_send, n_recv, out_sem,
    *, count, grad_scale,
):
    f32, bf16 = jnp.float32, jnp.bfloat16
    me = lax.axis_index("seq")
    core = lax.rem(me, 2)
    chip = lax.div(me, 2)
    chips = count // 2
    layers = count // 4
    partner = me + 1 - 2 * core
    side = lax.rem(chip, 2)
    layer = lax.div(chip, 2)
    share = D // count
    group = lax.axis_index("groups")
    mine_at = pl.multiple_of(core * ROWS, ROWS)
    other_at = pl.multiple_of((1 - core) * ROWS, ROWS)
    has_prev = chip > 0
    has_next = chip < chips - 1
    prev = lax.rem(me + count - 2, count)
    after = lax.rem(me + 2, count)

    def remote(source, target, send, recv, device, part_of=None):
        return pltpu.make_async_remote_copy(
            src_ref=source, dst_ref=target, send_sem=send, recv_sem=recv,
            device_id={"groups": group if part_of is None else part_of, "seq": device},
            device_id_type=pl.DeviceIdType.MESH,
        )

    def place(z, x, c):
        return (z * 2 + x) * 2 + c

    barrier = pltpu.get_barrier_semaphore()

    def greet(i, carry):
        pl.semaphore_signal(
            barrier, inc=1, device_id={"groups": group, "seq": lax.rem(me + 1 + i, count)},
            device_id_type=pl.DeviceIdType.MESH,
        )
        return carry

    lax.fori_loop(0, count - 1, greet, 0)
    pl.semaphore_signal(
        barrier, inc=1, device_id={"groups": 1 - group, "seq": me}, device_id_type=pl.DeviceIdType.MESH
    )

    for p in range(3):
        for h in range(2):
            wpack[p, h] = jnp.concatenate(
                [w_ref[:, t * D + h * HALF + p * PAIR : t * D + h * HALF + (p + 1) * PAIR] for t in range(3)],
                axis=1,
            )

    meta[0:1, :] = pos_ref[...]
    meta[1:2, :] = seg_ref[...]
    metag[2 + core] = meta[...]

    own_block = pl.ds(pl.multiple_of(me * share, share), share)
    for p in range(3):
        wg[p, own_block, :] = wpack[p, core]

    def block_of(device):
        return pl.ds(pl.multiple_of(device * share, share), share)

    def w_move(p, device, k, slot, to, part_of=None):
        rows = block_of(device)
        return remote(wg.at[p, rows, :], wg.at[p, rows, :], w_send.at[p, k], w_recv.at[p, slot], to, part_of)

    def hop_to(j):
        return lax.rem(layer + j, layers)

    def w_partner(p):
        return remote(
            wpack.at[p, 1 - core], wg.at[p, own_block, :], w_send.at[p, 0], w_recv.at[p, layer], partner
        )

    def w_near(p, j, c):
        return remote(
            wpack.at[p, c], wg.at[p, own_block, :], w_send.at[p, 2 * j - 1 + c], w_recv.at[p, layer],
            place(hop_to(j), side, c),
        )

    def w_cross(p, c):
        return remote(
            wpack.at[p, c], wg.at[p, own_block, :], w_send.at[p, 7 + c],
            w_recv.at[p, 2 * layers + layer], place(layer, 1 - side, c),
        )

    def w_around(p, j):
        return w_move(
            p, place(layer, 1 - side, group), 8 + j, 2 * layers + layer, place(hop_to(j), side, core)
        )

    def w_over_near(p, j):
        z = hop_to(j)
        return w_move(p, place(z, side, group), 11 + j, layers + z, me, 1 - group)

    def w_over_across(p, j):
        z = hop_to(j)
        return w_move(p, place(z, 1 - side, group), 15 + j, 3 * layers + z, me, 1 - group)

    def came(p, device, slot, part_of=None):
        w_move(p, device, 0, slot, partner, part_of).wait_recv()

    def loop(n, body):
        def step(i, carry):
            body(i)
            return carry

        lax.fori_loop(0, n, step, 0)

    def cross_weights(p):
        @pl.when(core == group)
        def _():
            for c in range(2):
                w_cross(p, c).start()

    def send_weights(p):
        w_partner(p).start()

        @pl.when(core == group)
        def _():
            for j in (2, 3, 1):
                for c in range(2):
                    w_near(p, j, c).start()

    def relay_first(p):
        came(p, place(layer, 1 - side, group), 2 * layers + layer)
        for j in (2, 3, 1):
            w_around(p, j).start()
        w_over_across(p, 0).start()

    def relay_near(p):
        for j in (1, 3, 2):
            came(p, place(hop_to(j), side, group), hop_to(j))
            w_over_near(p, j).start()

    def relay_across(p):
        for j in (1, 3, 2):
            came(p, place(hop_to(j), 1 - side, group), 2 * layers + hop_to(j))
            w_over_across(p, j).start()

    def await_weights(p):
        came(p, partner, layer)
        for j in range(1, layers):
            z = hop_to(j)
            came(p, place(z, side, 1 - group), layers + z)
        for j in range(layers):
            z = hop_to(j)
            came(p, place(z, 1 - side, 1 - group), 3 * layers + z)

    mine_rows = pl.ds(pl.multiple_of(W + mine_at, ROWS), ROWS)
    other_rows = pl.ds(pl.multiple_of(W + other_at, ROWS), ROWS)

    def chunk_rows(base, k):
        return pl.ds(pl.multiple_of(base + k * BLOCK, BLOCK), BLOCK)

    def x_swap():
        return remote(nx.at[mine_rows], nx.at[mine_rows], x_send.at[0], x_recv.at[0], partner)

    def x_swap_arrival():
        return remote(nx.at[other_rows], nx.at[other_rows], x_send.at[0], x_recv.at[0], partner)

    def x_next(k):
        n = 2 * k + core
        return remote(
            nx.at[chunk_rows(W, n)], nx.at[chunk_rows(0, n)], x_send.at[1 + k], x_recv.at[1 + k], after
        )

    def x_relay(k):
        rows = chunk_rows(0, 2 * k + core)
        return remote(nx.at[rows], nx.at[rows], x_send.at[3 + k], x_recv.at[3 + k], partner)

    def x_relay_arrival(k):
        rows = chunk_rows(0, 2 * k + 1 - core)
        return remote(nx.at[rows], nx.at[rows], x_send.at[3 + k], x_recv.at[3 + k], partner)

    def m_swap():
        return remote(metag.at[2 + core], metag.at[2 + core], m_send.at[0], m_recv.at[0], partner)

    def m_swap_arrival():
        return remote(metag.at[3 - core], metag.at[3 - core], m_send.at[0], m_recv.at[0], partner)

    def m_next(t):
        device = after - core + t
        return remote(meta, metag.at[core], m_send.at[1 + t], m_recv.at[1 + core], device)

    def m_prev_arrival(t):
        return remote(meta, metag.at[t], m_send.at[1 + t], m_recv.at[1 + t], prev)

    def g_swap():
        return remote(gsend, gbuf.at[pl.ds(mine_at, ROWS), :], g_send, g_recv, partner)

    def g_arrival():
        return remote(gsend, gbuf.at[pl.ds(other_at, ROWS), :], g_send, g_recv, partner)

    half_mine = pl.ds(pl.multiple_of(core * HALF, HALF), HALF)
    half_other = pl.ds(pl.multiple_of((1 - core) * HALF, HALF), HALF)
    gsend[...] = g_ref[:, half_other]
    gbuf[pl.ds(mine_at, ROWS), :] = g_ref[:, half_mine]

    def normalize(k):
        rows = pl.ds(pl.multiple_of(k * BLOCK, BLOCK), BLOCK)
        x = x_ref[rows, :].astype(f32)
        inv = lax.rsqrt(jnp.mean(x * x, axis=1, keepdims=True) + EPSILON)
        rms[rows, :] = inv
        nx[chunk_rows(W + mine_at, k), :] = (x * inv).astype(bf16)

    loop(2, normalize)

    pl.semaphore_wait(barrier, count)
    cross_weights(0)
    send_weights(0)
    cross_weights(1)
    cross_weights(2)
    m_swap().start()

    @pl.when(has_next)
    def _():
        m_next(0).start()
        m_next(1).start()

    x_swap().start()
    g_swap().start()

    relay_first(0)
    relay_near(0)
    x_swap_arrival().wait_recv()

    @pl.when(has_next)
    def _():
        x_next(1).start()
        x_next(0).start()

    send_weights(1)
    relay_first(1)
    relay_across(0)

    @pl.when(has_prev)
    def _():
        m_prev_arrival(0).wait_recv()
        m_prev_arrival(1).wait_recv()

    @pl.when(jnp.logical_not(has_prev))
    def _():
        row = lax.broadcasted_iota(jnp.int32, (8, ROWS), 0)
        gone = jnp.where(row == 1, -1, 0)
        metag[0] = gone
        metag[1] = gone
        nx[:W, :] = jnp.zeros((W, D), bf16)

    m_swap_arrival().wait_recv()
    g_arrival().wait_recv()

    index = lax.broadcasted_iota(jnp.int32, (TABLE, ROWS), 0)
    frequency = jnp.zeros((TABLE, ROWS), f32)
    for f, value in enumerate(frequencies()):
        frequency = jnp.where(index == f, value, frequency)
    for n in range(4):
        angle = metag[n][0:1, :].astype(f32) * frequency
        c, s = turn(angle)
        cosT[:, n * ROWS : (n + 1) * ROWS] = c
        sinT[:, n * ROWS : (n + 1) * ROWS] = s
        seg = metag[n][1:2, :].astype(f32)
        for j in range(ROWS // PAIR):
            flat = jnp.broadcast_to(seg[:, j * PAIR : (j + 1) * PAIR], (PAIR, PAIR))
            segc[n * ROWS + j * PAIR : n * ROWS + (j + 1) * PAIR, :] = jnp.transpose(flat)
    for n in range(2):
        gT[:, n * ROWS : (n + 1) * ROWS] = jnp.transpose(gbuf[n * ROWS : (n + 1) * ROWS, :])

    key = lax.broadcasted_iota(jnp.int32, (BLOCK, BLOCK), 0)
    query = lax.broadcasted_iota(jnp.int32, (BLOCK, BLOCK), 1)
    for b in range(W // BLOCK):
        at = b * BLOCK
        seg_q = metag[2 + at // ROWS][1:2, at % ROWS : at % ROWS + BLOCK].astype(f32)
        for c in range(SPAN // BLOCK):
            seg_k = segc[at + c * BLOCK : at + (c + 1) * BLOCK, :]
            same = jnp.concatenate([seg_k == seg_q[:, :PAIR], seg_k == seg_q[:, PAIR:]], axis=1)
            if c == 0:
                same = same & (key > query)
            if c == SPAN // BLOCK - 1:
                same = same & (key <= query)
            bias[b, c * BLOCK : (c + 1) * BLOCK, :] = jnp.where(same, 0.0, MASKED_SCORE)


    def table(n):
        cols = pl.ds(pl.multiple_of(n * BLOCK, BLOCK), BLOCK)
        return cols, cosT[:, cols], sinT[:, cols]

    def keep_kv(slot, cols, k, v):
        kT[slot, :, cols] = k
        vT[slot, :, cols] = v
        ks[slot, cols, :] = jnp.transpose(k)
        vs[slot, cols, :] = jnp.transpose(v)

    def project_before(slot, n):
        cols, c, s = table(n)
        kv = contract(wT[slot, PAIR:, :], nx[cols, :], 1, 1)
        keep_kv(slot, cols, rotated(kv[:PAIR], c, s).astype(bf16), kv[PAIR:].astype(bf16))

    def project_own(slot, i):
        cols, c, s = table(i + W // BLOCK)
        at = pl.ds(pl.multiple_of(i * BLOCK, BLOCK), BLOCK)
        qkv = contract(wT[slot], nx[cols, :], 1, 1)
        qT[slot, :, at] = rotated(qkv[:PAIR], c, s).astype(bf16) * bf16(SCORE_SCALE)
        k = rotated(qkv[PAIR : 2 * PAIR], c, s).astype(bf16)
        keep_kv(slot, cols, k, qkv[2 * PAIR :].astype(bf16))

    def finish_chunk(p, n):
        slot = lax.rem(p, 2)
        cols, c, s = table(n)
        k = rotated(dkT[slot, :, cols], c, -s).astype(bf16)
        v = dvT[slot, :, cols].astype(bf16)
        kv = jnp.concatenate([k, v], axis=0)
        dkvb[slot, :, cols] = kv
        dtok[p, cols, PAIR:] = jnp.transpose(kv)

    def finish_query(p, i):
        cols, c, s = table(i + W // BLOCK)
        at = pl.ds(pl.multiple_of(i * BLOCK, BLOCK), BLOCK)
        slot = lax.rem(p, 2)
        q = rotated(dqT[slot, :, at] * SCORE_SCALE, c, -s).astype(bf16)
        dqb[:, at] = q
        dtok[p, cols, :PAIR] = jnp.transpose(q)
        ctxs[p, at, :] = jnp.transpose(ctxT[slot, :, at])

    def ctx_copy(p):
        return remote(
            ctxs.at[p, pl.ds(other_at, ROWS), :], ctxr.at[p], ctx_send.at[p], ctx_recv.at[p], partner
        )

    deck = 2 * share

    def deck_rows(z, x):
        return pl.ds(pl.multiple_of((2 * z + x) * deck, deck), deck)

    def side_copy(p, z):
        return remote(
            part.at[p, deck_rows(z, 1 - side), :], sums.at[p, z], side_send.at[p, z], side_recv.at[p, z],
            place(layer, 1 - side, core),
        )

    def layer_copy(p, j):
        return remote(
            joined.at[p, j - 1], layered.at[p, j - 1], part_send.at[p, j - 1], part_recv.at[p, j - 1],
            place(hop_to(j), side, core),
        )

    def deck_copy(p):
        return remote(give.at[p], got.at[p], deck_send.at[p], deck_recv.at[p], partner)

    def both_sides(p, z):
        side_copy(p, z).wait_recv()
        return part[p, deck_rows(z, side), :].astype(f32) + sums[p, z].astype(f32)

    def join(p):
        for j in (2, 3, 1):
            joined[p, j - 1] = both_sides(p, hop_to(j)).astype(bf16)
            layer_copy(p, j).start()

    def share_out(p):
        total = both_sides(p, layer)
        for j in range(1, layers):
            layer_copy(p, j).wait_recv()
            total = total + layered[p, j - 1].astype(f32)
        decks[...] = total

        def rows(c):
            return decks[pl.ds(pl.multiple_of(c * share, share), share), :]

        give[p] = rows(1 - core).astype(bf16)
        deck_copy(p).start()
        kept[p] = rows(core)

    def collect(p):
        deck_copy(p).wait_recv()
        even = kept[p]
        odd = got[p].astype(f32)
        for t in range(3):
            at = t * D + p * PAIR
            a = pl.ds(pl.multiple_of(at + core * HALF, PAIR), PAIR)
            b = pl.ds(pl.multiple_of(at + (1 - core) * HALF, PAIR), PAIR)
            pg_ref[:, a] = even[:, t * PAIR : (t + 1) * PAIR] * grad_scale
            pg_ref[:, b] = odd[:, t * PAIR : (t + 1) * PAIR] * grad_scale

    def n_swap(k):
        return remote(ps.at[k], pr.at[k], n_send.at[k], n_recv.at[k], partner)

    def n_back(k):
        return remote(fwd.at[k], later.at[k], n_send.at[2 + k], n_recv.at[2 + k], prev)

    def n_own():
        return remote(ys, yr, n_send.at[4], n_recv.at[4], partner)

    def give_before(half, k):
        rows = chunk_rows(half * ROWS, k)
        mine = sum(contract(dtok[p, rows, PAIR:], wg[p, :, PAIR:], 1, 1) for p in range(3))

        @pl.when(core != half)
        def _():
            ps[k] = mine.astype(bf16)
            n_swap(k).start()

        @pl.when(core == half)
        def _():
            ngo[pl.ds(pl.multiple_of(k * BLOCK, BLOCK), BLOCK), :] = mine

    def pass_before(half, k):
        @pl.when(core == half)
        def _():
            n_swap(k).wait_recv()
            mine = ngo[pl.ds(pl.multiple_of(k * BLOCK, BLOCK), BLOCK), :]
            fwd[k] = (mine + pr[k].astype(f32)).astype(bf16)

            @pl.when(has_prev)
            def _():
                n_back(k).start()

    def own_grad(at, k):
        rows = chunk_rows(W + at, k)
        return sum(contract(dtok[p, rows, :], wg[p], 1, 1) for p in range(3))

    def begin(p, slot):
        await_weights(p)
        wT[slot] = jnp.transpose(wg[p])
        loop(4, lambda i: project_own(slot, i))
        dkT[slot] = jnp.zeros((PAIR, 2 * W), f32)
        dvT[slot] = jnp.zeros((PAIR, 2 * W), f32)

    def project_gradient(p):
        loop(4, lambda n: finish_chunk(p, n + 4))
        kv = contract(dkvb[lax.rem(p, 2)], nx[...], 1, 0)
        q = contract(dqb[...], nx[W:, :], 1, 0)
        part[p, :, :PAIR] = jnp.transpose(q.astype(bf16))
        part[p, :, PAIR:] = jnp.transpose(kv.astype(bf16))

    def send_gradient(p):
        for j in (2, 3, 1, 0):
            side_copy(p, hop_to(j)).start()
        ctx_copy(p).start()

    def relay_both(p):
        relay_near(p)
        relay_across(p)

    def step(t):
        p = jnp.where(t < 2, 0, jnp.where(t == 3, 2, 1))
        slot = lax.rem(p, 2)
        half = jnp.where((t == 0) | (t == 4), 1, 0)

        @pl.when((t == 0) | (t == 2) | (t == 3))
        def _():
            begin(p, slot)

        @pl.when((t < 2) & has_prev)
        def _():
            x_next(half).wait_recv()
            x_relay(half).start()
            x_relay_arrival(half).wait_recv()

        @pl.when(t < 2)
        def _():
            loop(2, lambda k: project_before(slot, half * 2 + k))

        @pl.when((t == 2) | (t == 3))
        def _():
            loop(4, lambda k: project_before(slot, k))

        @pl.when(((t == 1) & (side == 0)) | (t == 2))
        def _():
            relay_both(t)

        attend(
            [(p, slot, 2 * half), (p, slot, 2 * half + 1)],
            bias, qT, kT, vT, ks, vs, gT, ctxT, dqT, dkT, dvT,
        )

        @pl.when(t == 0)
        def _():
            relay_first(2)
            send_weights(2)

        @pl.when((t == 1) & (side == 1))
        def _():
            relay_both(1)

        @pl.when(t == 1)
        def _():
            loop(2, lambda n: finish_chunk(p, n))

        @pl.when((t == 1) | (t == 4))
        def _():
            loop(2, lambda n: finish_chunk(p, n + 2))
            loop(4, lambda n: finish_query(p, n))
            project_gradient(p)
            send_gradient(p)

        @pl.when(t == 2)
        def _():
            join(0)

        @pl.when(t == 3)
        def _():
            def finished(k):
                finish_chunk(1, k)
                finish_chunk(2, k)
                give_before(0, k)

            loop(2, finished)
            share_out(0)
            loop(2, lambda k: pass_before(0, k))

    loop(5, step)

    def last_step(k):
        attend([(2, 0, k + 2)], bias, qT, kT, vT, ks, vs, gT, ctxT, dqT, dkT, dvT)
        finish_chunk(2, k + 2)
        give_before(1, k)

        @pl.when(k == 0)
        def _():
            loop(2, lambda n: finish_query(2, n))

        finish_query(2, k + 2)
        pass_before(1, k)

    loop(2, last_step)
    project_gradient(2)
    send_gradient(2)

    def give_own(k):
        ys[pl.ds(pl.multiple_of(k * BLOCK, BLOCK), BLOCK), :] = own_grad(other_at, k).astype(bf16)

    loop(2, give_own)
    n_own().start()

    def keep_own(k):
        ngo[pl.ds(pl.multiple_of(k * BLOCK, BLOCK), BLOCK), :] = own_grad(mine_at, k)

    loop(2, keep_own)

    for p in range(3):
        ctx_copy(p).wait()
        mine_cols = pl.ds(pl.multiple_of(core * HALF + p * PAIR, PAIR), PAIR)
        other_cols = pl.ds(pl.multiple_of((1 - core) * HALF + p * PAIR, PAIR), PAIR)
        ctx_ref[:, mine_cols] = ctxs[p, pl.ds(mine_at, ROWS), :]
        ctx_ref[:, other_cols] = ctxr[p]

    ctx_leaves = pltpu.make_async_copy(ctx_ref, ctx_out, out_sem.at[0])
    ctx_leaves.start()

    m_swap().wait_send()
    x_swap().wait_send()
    g_swap().wait_send()

    @pl.when(has_next)
    def _():
        for k in range(2):
            m_next(k).wait_send()
            x_next(k).wait_send()

    @pl.when(has_prev)
    def _():
        for k in range(2):
            x_relay(k).wait_send()

    for p in range(3):
        w_partner(p).wait_send()
        w_over_across(p, 0).wait_send()
        for j in range(1, layers):
            w_around(p, j).wait_send()
            w_over_near(p, j).wait_send()
            w_over_across(p, j).wait_send()

        @pl.when(core == group)
        def _():
            for c in range(2):
                w_cross(p, c).wait_send()
                for j in range(1, layers):
                    w_near(p, j, c).wait_send()

    join(1)
    join(2)

    collect(0)
    share_out(1)
    share_out(2)
    collect(1)
    n_own().wait()

    @pl.when(has_next)
    def _():
        n_back(0).wait_recv()
        n_back(1).wait_recv()

    @pl.when(jnp.logical_not(has_next))
    def _():
        later[...] = jnp.zeros_like(later)

    def finish(k):
        rows = pl.ds(pl.multiple_of(k * BLOCK, BLOCK), BLOCK)
        ng = ngo[rows, :] + yr[rows, :].astype(f32) + later[k].astype(f32)
        inv = rms[rows, :]
        scaled = x_ref[rows, :].astype(f32) * inv
        ig_ref[rows, :] = (
            inv * (ng - scaled * jnp.mean(ng * scaled, axis=1, keepdims=True))
        ).astype(bf16)

    loop(2, finish)
    ig_leaves = pltpu.make_async_copy(ig_ref, ig_out, out_sem.at[1])
    ig_leaves.start()
    collect(2)
    pg_leaves = pltpu.make_async_copy(pg_ref, pg_out, out_sem.at[2])
    pg_leaves.start()

    for p in range(3):
        for j in range(1, layers):
            layer_copy(p, j).wait_send()
        for z in range(layers):
            side_copy(p, z).wait_send()
        deck_copy(p).wait_send()

    @pl.when(has_prev)
    def _():
        for k in range(2):
            n_back(k).wait_send()

    for k in range(2):
        n_swap(k).wait_send()
    ctx_leaves.wait()
    ig_leaves.wait()
    pg_leaves.wait()


def hand_over_kernel(*refs):
    sources, targets, held, sems = refs[:3], refs[3:6], refs[6:9], refs[9]
    arrive = [pltpu.make_async_copy(sources[n], held[n], sems.at[n]) for n in range(3)]
    leave = [pltpu.make_async_copy(held[n], targets[n], sems.at[3 + n]) for n in range(3)]
    for copy in arrive:
        copy.start()
    for n in range(3):
        arrive[n].wait()
        leave[n].start()
    for copy in leave:
        copy.wait()


def hand_over(*arrays):
    anywhere = pl.BlockSpec(memory_space=pl.ANY)
    return pl.pallas_call(
        hand_over_kernel,
        out_shape=[jax.ShapeDtypeStruct(a.shape, a.dtype) for a in arrays],
        in_specs=[anywhere] * 3,
        out_specs=[anywhere] * 3,
        scratch_shapes=[pltpu.VMEM(a.shape, a.dtype) for a in arrays] + [pltpu.SemaphoreType.DMA((6,))],
        name="hand_over",
    )(*arrays)


def whole(count, grad_scale, x, weights, positions, segments, out_grads):
    share = D // count
    bf16, f32 = jnp.bfloat16, jnp.float32
    total = 2 * W
    vmem = pl.BlockSpec(memory_space=pltpu.VMEM)
    dma = pltpu.SemaphoreType.DMA
    layers = count // 4
    return pl.pallas_call(
        functools.partial(whole_kernel, count=count, grad_scale=grad_scale),
        out_shape=[
            jax.ShapeDtypeStruct((ROWS, D), bf16),
            jax.ShapeDtypeStruct((ROWS, D), bf16),
            jax.ShapeDtypeStruct((share, 3 * D), f32),
        ],
        in_specs=[vmem] * 5,
        out_specs=[pl.BlockSpec(memory_space=pl.ANY)] * 3,
        scratch_shapes=[
            pltpu.VMEM((ROWS, D), bf16),
            pltpu.VMEM((ROWS, D), bf16),
            pltpu.VMEM((share, 3 * D), f32),
            pltpu.VMEM((total, D), bf16),
            pltpu.VMEM((ROWS, 1), f32),
            pltpu.VMEM((3, D, 3 * PAIR), bf16),
            pltpu.VMEM((3, 2, share, 3 * PAIR), bf16),
            pltpu.VMEM((2, 3 * PAIR, D), bf16),
            pltpu.VMEM((8, ROWS), jnp.int32),
            pltpu.VMEM((4, 8, ROWS), jnp.int32),
            pltpu.VMEM((ROWS, HALF), bf16),
            pltpu.VMEM((W, HALF), bf16),
            pltpu.VMEM((HALF, W), bf16),
            pltpu.VMEM((TABLE, total), f32),
            pltpu.VMEM((TABLE, total), f32),
            pltpu.VMEM((total, PAIR), f32),
            pltpu.VMEM((W // BLOCK, SPAN, BLOCK), f32),
            pltpu.VMEM((2, PAIR, W), bf16),
            pltpu.VMEM((2, PAIR, total), bf16),
            pltpu.VMEM((2, PAIR, total), bf16),
            pltpu.VMEM((2, total, PAIR), bf16),
            pltpu.VMEM((2, total, PAIR), bf16),
            pltpu.VMEM((2, PAIR, W), bf16),
            pltpu.VMEM((2, PAIR, W), f32),
            pltpu.VMEM((2, PAIR, total), f32),
            pltpu.VMEM((2, PAIR, total), f32),
            pltpu.VMEM((PAIR, W), bf16),
            pltpu.VMEM((2, 2 * PAIR, total), bf16),
            pltpu.VMEM((3, total, 3 * PAIR), bf16),
            pltpu.VMEM((3, W, PAIR), bf16),
            pltpu.VMEM((3, ROWS, PAIR), bf16),
            pltpu.VMEM((3, D, 3 * PAIR), bf16),
            pltpu.VMEM((3, layers, 2 * share, 3 * PAIR), bf16),
            pltpu.VMEM((3, layers - 1, 2 * share, 3 * PAIR), bf16),
            pltpu.VMEM((3, layers - 1, 2 * share, 3 * PAIR), bf16),
            pltpu.VMEM((2 * share, 3 * PAIR), f32),
            pltpu.VMEM((3, share, 3 * PAIR), f32),
            pltpu.VMEM((3, share, 3 * PAIR), bf16),
            pltpu.VMEM((3, share, 3 * PAIR), bf16),
            pltpu.VMEM((2, BLOCK, D), bf16),
            pltpu.VMEM((2, BLOCK, D), bf16),
            pltpu.VMEM((2, BLOCK, D), bf16),
            pltpu.VMEM((2, BLOCK, D), bf16),
            pltpu.VMEM((ROWS, D), bf16),
            pltpu.VMEM((ROWS, D), bf16),
            pltpu.VMEM((ROWS, D), f32),
            dma((3, 15 + layers)), dma((3, 4 * layers)),
            dma((5,)), dma((5,)),
            dma((3,)), dma((3,)),
            dma, dma,
            dma((3, layers)), dma((3, layers)),
            dma((3, layers - 1)), dma((3, layers - 1)),
            dma((3,)), dma((3,)),
            dma((3,)), dma((3,)),
            dma((5,)), dma((5,)),
            dma((3,)),
        ],
        compiler_params=pltpu.CompilerParams(
            vmem_limit_bytes=60 * 1024 * 1024, collective_id=0, has_side_effects=True
        ),
        name="whole_sublayer",
    )(x, weights, positions, segments, out_grads)


def swapped(value):
    count = lax.axis_size("seq")
    return lax.ppermute(value, "seq", [(s, s ^ 1) for s in range(count)])


def chip_shifted(value, steps):
    count = lax.axis_size("seq")
    pairs = [(s, s + 2 * steps) for s in range(count) if 0 <= s + 2 * steps < count]
    return lax.ppermute(value, "seq", pairs)


def ordered(core, mine, other, axis=0):
    first = jnp.where(core == 0, mine, other)
    second = jnp.where(core == 0, other, mine)
    return jnp.concatenate([first, second], axis=axis)


def local(inputs, projection, positions, segments, context_grad):
    row_count = inputs.shape[0]
    device_count = lax.axis_size("seq")
    chips = device_count // 2
    device_index = lax.axis_index("seq")
    core = device_index % 2
    chip = device_index // 2
    assert 2 * row_count == W
    grad_scale = (row_count * device_count) ** (-0.5)

    if device_count == 16 and lax.axis_size("groups") == 2:
        return tuple(
            hand_over(
                *whole(
                    device_count, grad_scale, inputs, projection, positions[None, :], segments[None, :],
                    context_grad,
                )
            )
        )

    weights = lax.all_gather(projection, "seq", axis=0, tiled=True)

    meta = jnp.stack([positions, segments], axis=0)
    x_before = chip_shifted(inputs, 1)
    meta_before = chip_shifted(meta, 1)
    x_other = swapped(inputs)
    meta_other = swapped(meta)
    x_before_other = swapped(x_before)
    meta_before_other = swapped(meta_before)
    grad_mine = lax.dynamic_slice_in_dim(context_grad, core * HALF, HALF, 1)
    grad_sent = lax.dynamic_slice_in_dim(context_grad, (1 - core) * HALF, HALF, 1)
    grad_other = swapped(grad_sent)
    out_grads = ordered(core, grad_mine, grad_other)

    x_all = jnp.concatenate(
        [ordered(core, x_before, x_before_other), ordered(core, inputs, x_other)], axis=0
    ).astype(jnp.float32)
    nx = (
        x_all * lax.rsqrt(jnp.mean(x_all * x_all, axis=1, keepdims=True) + EPSILON)
    ).astype(jnp.bfloat16)
    meta_all = jnp.concatenate(
        [ordered(core, meta_before, meta_before_other, 1), ordered(core, meta, meta_other, 1)],
        axis=1,
    )
    half_size = HD // 2
    frequency = jnp.exp(-math.log(10000.0) * jnp.arange(half_size, dtype=jnp.float32) / half_size)
    angle = meta_all[0].astype(jnp.float32)[:, None] * frequency[None, :]
    c, s = jnp.cos(angle), jnp.sin(angle)
    cosine = jnp.concatenate([c, c, c, c], axis=1)
    sine = jnp.concatenate([-s, s, -s, s], axis=1)
    seg_all = meta_all[1]
    outside = (jnp.arange(seg_all.shape[0]) < W) & (chip == 0)
    seg_k = jnp.where(outside, -1, seg_all)[None, :]
    seg_q = seg_all[W:][:, None]

    x_float = inputs.astype(jnp.float32)
    inv_rms = lax.rsqrt(jnp.mean(x_float * x_float, axis=1, keepdims=True) + EPSILON)
    scaled = x_float * inv_rms

    context_heads, dq, dk, dv = attention(
        core.astype(jnp.int32)[None], nx, weights, cosine, sine, seg_q, seg_k, out_grads
    )

    mine_at = core * row_count
    other_at = (1 - core) * row_count
    context_mine = lax.dynamic_slice_in_dim(context_heads, mine_at, row_count, 0)
    context_other = swapped(lax.dynamic_slice_in_dim(context_heads, other_at, row_count, 0))
    context = ordered(core, context_mine, context_other, 1)

    w_q, w_k, w_v = [
        lax.dynamic_slice_in_dim(weights, t * D + core * HALF, HALF, 1) for t in range(3)
    ]
    dkv = jnp.concatenate([dk, dv], axis=1)
    w_kv = jnp.concatenate([w_k, w_v], axis=1)
    ng_kv = contract(dkv, w_kv, 1, 1)
    ng_q = contract(dq, w_q, 1, 1)
    ng_before = ng_kv[:W]
    ng_own = ng_kv[W:] + ng_q
    send_before = lax.dynamic_slice_in_dim(ng_before, other_at, row_count, 0).astype(jnp.bfloat16)
    keep_before = lax.dynamic_slice_in_dim(ng_before, mine_at, row_count, 0)
    before = keep_before + swapped(send_before).astype(jnp.float32)
    later = chip_shifted(before.astype(jnp.bfloat16), -1)
    send_own = lax.dynamic_slice_in_dim(ng_own, other_at, row_count, 0).astype(jnp.bfloat16)
    keep_own = lax.dynamic_slice_in_dim(ng_own, mine_at, row_count, 0)
    normed_grad = (
        keep_own + swapped(send_own).astype(jnp.float32) + later.astype(jnp.float32)
    )
    input_grad = (
        inv_rms * (normed_grad - scaled * jnp.mean(normed_grad * scaled, axis=1, keepdims=True))
    ).astype(jnp.bfloat16)

    pg_kv = contract(nx, dkv, 0, 0)
    pg_q = contract(nx[W:], dq, 0, 0)
    pg = jnp.concatenate([pg_q, pg_kv], axis=1).astype(jnp.bfloat16)
    groups = [[2 * i + k for i in range(chips)] for k in range(2)]
    summed = lax.psum_scatter(
        pg, "seq", scatter_dimension=0, axis_index_groups=groups, tiled=True
    ).astype(jnp.float32)
    rows = summed.shape[0] // 2
    keep = lax.dynamic_slice_in_dim(summed, core * rows, rows, 0)
    other = swapped(lax.dynamic_slice_in_dim(summed, (1 - core) * rows, rows, 0).astype(jnp.bfloat16))
    other = other.astype(jnp.float32)
    parts = []
    for t in range(3):
        cols = slice(t * HALF, (t + 1) * HALF)
        parts.append(ordered(core, keep[:, cols], other[:, cols], 1))
    projection_grad = jnp.concatenate(parts, axis=1) * grad_scale
    return (context, input_grad, projection_grad)


def solution(mesh):
    in_specs = (
        P(("groups", "seq"), None),
        P("seq", None),
        P(("groups", "seq")),
        P(("groups", "seq")),
        P(("groups", "seq"), None),
    )
    out_specs = (P(("groups", "seq"), None), P(("groups", "seq"), None), P(("groups", "seq"), None))
    return jax.shard_map(local, mesh=mesh, in_specs=in_specs, out_specs=out_specs, check_vma=False)
```
